128 devices in a mesh: rows: 32 (over x, z, core), cols: 4 (over y).
Axes of the slice: x: 4, y: 4, z: 4, core: 2. Of those that a mesh axis runs over, the one named last changes fastest.
Arguments:
- basis: bfloat16 [262144, 512], P('rows', 'cols'), may hold values from -6 to 6
- lower: bfloat16 [1024, 256, 256], P('rows'), may hold values from -0.375 to 0.375
- diag: bfloat16 [1024, 256, 256], P('rows'), may hold values from -0.375 to 0.375
- upper: bfloat16 [1024, 256, 256], P('rows'), may hold values from -0.375 to 0.375
- inverse: bfloat16 [1024, 256, 256], P('rows'), may hold values from -0.375 to 0.375
Outputs:
- ortho: bfloat16 [262144, 512], P('rows', 'cols')
- projected: float32 [512, 512], P(None, 'cols')
The draws below stay inside these ranges and needn't reach their ends.
All inputs are finite; a program needn't handle non-finite values.
Results may differ from the reference program's by a relative error of at most 0.0085.
Values may be sent and summed in bfloat16 or wider, within the bound.
No kernel may reach another device: no remote copies, remote signals or barrier semaphores. Data moves between devices by JAX's collectives and lax.ppermute only.
A program may use at most 128 MiB of HBM per device.

```python
import jax
import jax.numpy as jnp
from jax import lax

BS = 256
K = 512
NB = 1024
ORDER = 262144


def block_scale(stream_key, shape, shards, low, largest):
    def one(dim, shards_of):
        heights = jax.random.uniform(jax.random.fold_in(jax.random.fold_in(stream_key, 6), dim), (shards_of,), jnp.float32, low / len(shards), largest / len(shards))
        return jnp.repeat(jnp.exp(heights), shape[dim] // shards_of).reshape((-1,) + (1,) * (len(shape) - dim - 1))

    gain = one(*shards[0])
    for cut in shards[1:]:
        gain = gain * one(*cut)
    return gain


def scatter_about(key, extent, scale, reach, pieces=(), kind=jnp.bfloat16):
    array = scale * jax.random.normal(key, extent, jnp.float32)
    if pieces:
        array = array * block_scale(key, extent, pieces, -0.22, 0.18)
    return jnp.clip(array, -reach, reach).astype(kind)


def setup_inputs(seed: int = 0) -> dict:
    streams_of = jax.random.split(jax.random.key(seed), 6)
    return {
        "basis": scatter_about(streams_of[0], (ORDER, K), 1.0, 6.0, ((0, 32), (1, 4))),
        "lower": scatter_about(streams_of[1], (NB, BS, BS), BS ** -0.5, 0.375, ((0, 32),)),
        "diag": scatter_about(streams_of[2], (NB, BS, BS), BS ** -0.5, 0.375, ((0, 32),)),
        "upper": scatter_about(streams_of[3], (NB, BS, BS), BS ** -0.5, 0.375, ((0, 32),)),
        "inverse": scatter_about(streams_of[4], (NB, BS, BS), BS ** -0.5, 0.375, ((0, 32),)),
    }


def operate(field, lower, diag, upper, inverse):
    blocks = field.reshape(NB, BS, K).astype(jnp.float32)
    zero = jnp.zeros((1, BS, K), jnp.float32)
    before = jnp.concatenate([zero, blocks[:-1]], axis=0)
    after = jnp.concatenate([blocks[1:], zero], axis=0)
    mixed = jnp.einsum('bij,bjc->bic', lower.astype(jnp.float32), before)
    mixed = mixed + jnp.einsum('bij,bjc->bic', diag.astype(jnp.float32), blocks)
    mixed = mixed + jnp.einsum('bij,bjc->bic', upper.astype(jnp.float32), after)
    mixed = mixed.astype(jnp.bfloat16).astype(jnp.float32)
    result = jnp.einsum('bij,bjc->bic', inverse.astype(jnp.float32), mixed)
    return result.astype(jnp.bfloat16).reshape(NB * BS, K)

def reference(basis, lower, diag, upper, inverse):
    work = operate(basis, lower, diag, upper, inverse)
    gram = jnp.dot(work.T.astype(jnp.float32), work.astype(jnp.float32), preferred_element_type=jnp.float32)
    factor = jnp.linalg.cholesky(gram)
    identity = jnp.eye(K, dtype=jnp.float32)
    linv = lax.linalg.triangular_solve(factor, identity, left_side=True, lower=True)
    rinv = linv.T.astype(jnp.bfloat16)
    ortho = jnp.dot(work.astype(jnp.float32), rinv.astype(jnp.float32), preferred_element_type=jnp.float32).astype(jnp.bfloat16)
    image = operate(ortho, lower, diag, upper, inverse)
    projected = jnp.dot(ortho.T.astype(jnp.float32), image.astype(jnp.float32), preferred_element_type=jnp.float32)
    return (ortho, projected)
```

```python
import functools

import jax
import jax.numpy as jnp
from jax import lax
from jax.experimental import pallas as pl
from jax.experimental.pallas import tpu as pltpu
from jax.sharding import PartitionSpec as P

F32 = jnp.float32
BF16 = jnp.bfloat16
HI = lax.Precision.HIGHEST
X, Z, CORE, Y = 4, 4, 2, 4
PARTS = 4
LIMIT = 56 << 20


def dot(a, b, ca=1, cb=0, precision=None):
    return lax.dot_general(
        a, b, (((ca,), (cb,)), ((), ())), precision=precision, preferred_element_type=F32
    )


def vmem():
    return pl.BlockSpec(memory_space=pltpu.VMEM)


def shape(dims, dtype):
    return jax.ShapeDtypeStruct(dims, dtype)


def over_rows(move):
    pairs = []
    for x in range(X):
        for z in range(Z):
            for core in range(CORE):
                tx, tz, tc = move(x, z, core)
                source = (x * Z + z) * CORE + core
                pairs.append((source, ((tx % X) * Z + tz % Z) * CORE + tc % CORE))
    return pairs


def flip(value):
    return lax.ppermute(value, "rows", over_rows(lambda x, z, c: (x, z, c + 1)))


def first_axis(value, s):
    return lax.ppermute(
        value, "rows", over_rows(lambda x, z, c: (x + s * (1 - c), z + s * c, c))
    )


def second_axis(value, s):
    return lax.ppermute(
        value, "rows", over_rows(lambda x, z, c: (x + s * c, z + s * (1 - c), c))
    )


def along_cols(value, s):
    return lax.ppermute(value, "cols", [(i, (i + s) % Y) for i in range(Y)])


def chain(value, step):
    count = X * Z * CORE * Y
    return lax.ppermute(
        value,
        ("rows", "cols"),
        [(i, i + step) for i in range(count) if 0 <= i + step < count],
    )


def reduce_all(keep, send):
    got = flip(send)
    q = keep.shape[0] // PARTS
    piece = [keep[t * q : (t + 1) * q] + got[t * q : (t + 1) * q] for t in range(PARTS)]
    r1, r2, r3 = (first_axis(piece[s], s) for s in (1, 2, 3))
    total = (piece[0] + r2) + (r1 + r3)
    r1, r2, r3 = (second_axis(total, s) for s in (1, 2, 3))
    total = (total + r2) + (r1 + r3)
    r1, r2, r3 = (along_cols(total, s) for s in (1, 2, 3))
    total = (total + r2) + (r1 + r3)
    other = flip(total)
    mine = [total] + [first_axis(total, s) for s in (3, 2, 1)]
    rest = [other] + [second_axis(other, s) for s in (3, 2, 1)]
    return mine + rest


def place(meta, pieces, flat):
    core = meta[1]
    q = pieces[0].shape[0]
    for which in range(2):
        half = core if which == 0 else 1 - core
        index = jnp.where(half == 0, meta[2], meta[3])
        for t in range(PARTS):
            at = (half * PARTS + lax.rem(index + t, PARTS)) * q
            flat[pl.ds(pl.multiple_of(at, q), q), :] = pieces[which * PARTS + t][...]


def split(meta, flat, keep, send):
    core = meta[1]
    q = flat.shape[0] // (2 * PARTS)
    for which, out in enumerate((keep, send)):
        half = core if which == 0 else 1 - core
        index = jnp.where(half == 0, meta[2], meta[3])
        for t in range(PARTS):
            at = (half * PARTS + lax.rem(index + t, PARTS)) * q
            out[t * q : (t + 1) * q, :] = flat[pl.ds(pl.multiple_of(at, q), q), :]


def one_block(before, here, after, lower, diag, upper, inverse):
    mixed = dot(lower, before) + dot(diag, here) + dot(upper, after)
    return dot(inverse, mixed.astype(BF16)).astype(BF16)


def op_kernel(meta, prev, cur, nxt, low, high, lower, diag, upper, inverse, out, *, j, per, count):
    size = diag.shape[1]
    first = lax.rem(meta[0] + j, Y) * (count // Y) + pl.program_id(0) * per
    v = [jnp.where(first == 0, low[...], prev[...])]
    v += [cur[k * size : (k + 1) * size, :] for k in range(per)]
    v += [jnp.where(first + per == count, high[...], nxt[...])]
    for k in range(per):
        out[k * size : (k + 1) * size, :] = one_block(
            v[k], v[k + 1], v[k + 2], lower[k], diag[k], upper[k], inverse[k]
        )


def op_chunk(meta, basis, low, high, lower, diag, upper, inverse, j):
    count, size, _ = diag.shape
    width = basis.shape[1]
    per = 2
    steps = count // Y // per

    def block(i, m):
        return lax.rem(m[0] + j, Y) * steps + i

    def at(i, m):
        return (block(i, m), 0)

    def weights(i, m):
        return (block(i, m), 0, 0)

    mat = pl.BlockSpec((per, size, size), weights)
    return pl.pallas_call(
        functools.partial(op_kernel, j=j, per=per, count=count),
        out_shape=shape((count // Y * size, width), BF16),
        grid_spec=pltpu.PrefetchScalarGridSpec(
            num_scalar_prefetch=1,
            grid=(steps,),
            in_specs=[
                pl.BlockSpec((size, width), lambda i, m: (jnp.maximum(block(i, m) * per - 1, 0), 0)),
                pl.BlockSpec((per * size, width), at),
                pl.BlockSpec(
                    (size, width), lambda i, m: (jnp.minimum(block(i, m) * per + per, count - 1), 0)
                ),
                pl.BlockSpec((size, width), lambda i, m: (0, 0)),
                pl.BlockSpec((size, width), lambda i, m: (0, 0)),
                mat,
                mat,
                mat,
                mat,
            ],
            out_specs=pl.BlockSpec((per * size, width), lambda i, m: (i, 0)),
        ),
        compiler_params=pltpu.CompilerParams(vmem_limit_bytes=LIMIT),
        name=f"op{j}",
    )(meta, basis, basis, basis, low, high, lower, diag, upper, inverse)


def gram_kernel(meta, p0, p1, p2, p3, wide, top, bottom, keep, send, full, flat, *, size):
    width = p0.shape[1]
    for s, piece in enumerate((p0, p1, p2, p3)):
        at = lax.rem(meta[0] + Y - s, Y) * width
        wide[:, pl.ds(pl.multiple_of(at, width), width)] = piece[...]
    rows = wide.shape[0]
    top[...] = wide[0:size, :]
    bottom[...] = wide[rows - size : rows, :]
    full[...] = dot(wide[...], wide[...], 0, 0)
    n = 0
    for a in range(Y):
        for b in range(a, Y):
            flat[n * width : (n + 1) * width, :] = full[
                a * width : (a + 1) * width, b * width : (b + 1) * width
            ]
            n += 1
    split(meta, flat, keep, send)


def gram_of(meta, pieces, size):
    rows, width = pieces[0].shape
    k = Y * width
    n = Y * (Y + 1) // 2 * width
    return pl.pallas_call(
        functools.partial(gram_kernel, size=size),
        out_shape=(
            shape((rows, k), BF16),
            shape((size, k), BF16),
            shape((size, k), BF16),
            shape((n // 2, width), F32),
            shape((n // 2, width), F32),
        ),
        grid_spec=pltpu.PrefetchScalarGridSpec(
            num_scalar_prefetch=1,
            in_specs=[vmem()] * 4,
            out_specs=(vmem(),) * 5,
            scratch_shapes=[pltpu.VMEM((k, k), F32), pltpu.VMEM((n, width), F32)],
        ),
        compiler_params=pltpu.CompilerParams(vmem_limit_bytes=LIMIT),
        name="gram",
    )(meta, *pieces)


def moment_kernel(meta, prev, cur, nxt, low, high, lower, diag, upper, inverse, keep, send, acc, flat):
    i = pl.program_id(0)
    last = pl.num_programs(0) - 1
    before = jnp.where(i == 0, low[...], prev[...])
    after = jnp.where(i == last, high[...], nxt[...])
    here = cur[...]
    image = one_block(before, here, after, lower[0], diag[0], upper[0], inverse[0])
    term = dot(here, image, 0, 0)

    @pl.when(i == 0)
    def _():
        acc[...] = term

    @pl.when(i > 0)
    def _():
        acc[...] += term

    @pl.when(i == last)
    def _():
        k = acc.shape[0]
        width = k // Y
        for b in range(Y):
            flat[b * k : (b + 1) * k, :] = acc[:, b * width : (b + 1) * width]
        split(meta, flat, keep, send)


def moment_of(meta, wide, low, high, lower, diag, upper, inverse):
    count, size, _ = diag.shape
    steps = count // Y
    k = wide.shape[1]
    width = k // Y
    n = Y * k
    mat = pl.BlockSpec((1, size, size), lambda i, m: (m[0] * steps + i, 0, 0))
    out = pl.BlockSpec((n // 2, width), lambda i, m: (0, 0))
    return pl.pallas_call(
        moment_kernel,
        out_shape=(shape((n // 2, width), F32), shape((n // 2, width), F32)),
        grid_spec=pltpu.PrefetchScalarGridSpec(
            num_scalar_prefetch=1,
            grid=(steps,),
            in_specs=[
                pl.BlockSpec((size, k), lambda i, m: (jnp.maximum(i - 1, 0), 0)),
                pl.BlockSpec((size, k), lambda i, m: (i, 0)),
                pl.BlockSpec((size, k), lambda i, m: (jnp.minimum(i + 1, steps - 1), 0)),
                pl.BlockSpec((size, k), lambda i, m: (0, 0)),
                pl.BlockSpec((size, k), lambda i, m: (0, 0)),
                mat,
                mat,
                mat,
                mat,
            ],
            out_specs=(out, out),
            scratch_shapes=[pltpu.VMEM((k, k), F32), pltpu.VMEM((n, width), F32)],
        ),
        compiler_params=pltpu.CompilerParams(vmem_limit_bytes=LIMIT),
        name="moment",
    )(meta, wide, wide, wide, low, high, lower, diag, upper, inverse)


def eliminate(a):
    groups = len(a)
    wide = (8, 8 * groups)
    sub = lax.broadcasted_iota(jnp.int32, wide, 0)
    lane = lax.broadcasted_iota(jnp.int32, wide, 1)
    a = list(a)
    e = [jnp.where(lane == sub + 8 * g, 1.0, 0.0).astype(F32) for g in range(groups)]

    def column(value, k):
        return jnp.broadcast_to(value[:, k : k + 1], wide)

    def row(value, k):
        return jnp.broadcast_to(value[k : k + 1, :], wide)

    for g in range(groups):
        base = 8 * g
        cols = [column(a[g], base + k) for k in range(8)]
        d = [[row(cols[k], i) if i >= k else None for k in range(8)] for i in range(8)]
        low = [[None] * 8 for _ in range(8)]
        scale = [None] * 8
        for k in range(8):
            scale[k] = lax.rsqrt(d[k][k])
            for i in range(k + 1, 8):
                low[i][k] = d[i][k] * scale[k]
            for i in range(k + 1, 8):
                for j in range(k + 1, i + 1):
                    d[i][j] = d[i][j] - low[i][k] * low[j][k]

        def forward(value):
            out = []
            for k in range(8):
                x = value[k]
                for j in range(k):
                    x = x - low[k][j] * out[j]
                out.append(x * scale[k])
            return out

        ra = forward([row(a[g], k) for k in range(8)]) if g + 1 < groups else None
        re = forward([row(e[g], k) for k in range(8)])
        for h in range(g + 1, groups):
            f = forward([column(a[h], base + k) for k in range(8)])
            for k in range(8):
                a[h] = a[h] - f[k] * ra[k]
                e[h] = e[h] - f[k] * re[k]
        rows = re[0]
        for k in range(1, 8):
            rows = jnp.where(sub == k, re[k], rows)
        e[g] = rows
    return e


def factor_kernel(meta, *refs):
    pieces, (out, w, inv, flat) = refs[: 2 * PARTS], refs[2 * PARTS :]
    n = w.shape[0]
    nb = n // Y
    place(meta, pieces, flat)
    at = 0
    for a in range(Y):
        for b in range(a, Y):
            block = flat[at : at + nb, :]
            w[a * nb : (a + 1) * nb, b * nb : (b + 1) * nb] = block
            if a != b:
                w[b * nb : (b + 1) * nb, a * nb : (a + 1) * nb] = block.T
            at += nb
    for p in range(Y):
        lo, hi = p * nb, (p + 1) * nb
        li = jnp.concatenate(
            eliminate([w[lo + 8 * g : lo + 8 * g + 8, lo:hi] for g in range(nb // 8)]), axis=0
        )
        if p:
            inv[lo:hi, 0:lo] = dot(li, inv[lo:hi, 0:lo], precision=HI)
        inv[lo:hi, lo:hi] = li
        if hi < n:
            inv[lo:hi, hi:n] = jnp.zeros((nb, n - hi), F32)
            l21 = dot(w[hi:n, lo:hi], li, 1, 1, HI)
            r12 = dot(li, w[lo:hi, hi:n], precision=HI)
            w[hi:n, hi:n] = w[hi:n, hi:n] - dot(l21, r12, precision=HI)
            new = dot(l21, inv[lo:hi, 0:hi], precision=HI)
            if p:
                inv[hi:n, 0:lo] = inv[hi:n, 0:lo] - new[:, 0:lo]
            inv[hi:n, lo:hi] = -new[:, lo:hi]
    out[...] = inv[...].astype(BF16)


def factor_of(meta, pieces):
    q, width = pieces[0].shape
    k = Y * width
    return pl.pallas_call(
        factor_kernel,
        out_shape=shape((k, k), BF16),
        grid_spec=pltpu.PrefetchScalarGridSpec(
            num_scalar_prefetch=1,
            in_specs=[vmem()] * (2 * PARTS),
            out_specs=vmem(),
            scratch_shapes=[
                pltpu.VMEM((k, k), F32),
                pltpu.VMEM((k, k), F32),
                pltpu.VMEM((2 * PARTS * q, width), F32),
            ],
        ),
        compiler_params=pltpu.CompilerParams(vmem_limit_bytes=LIMIT),
        name="factor",
    )(meta, *pieces)


def ortho_kernel(meta, linv, p0, p1, p2, p3, *refs):
    out = refs[-1]
    width = p0.shape[1]
    c = meta[0]
    mine = pl.ds(pl.multiple_of(c * width, width), width)
    parts = []
    for s in range(Y):
        at = pl.multiple_of(lax.rem(c + Y - s, Y) * width, width)
        parts.append(linv[mine, pl.ds(at, width)])
    left = jnp.concatenate([p0[...], p1[...], p2[...], p3[...]], axis=1)
    out[...] = dot(left, jnp.concatenate(parts, axis=1), 1, 1).astype(BF16)


def ortho_chunk(meta, linv, pieces, into, i):
    rows, width = pieces[0].shape
    k = linv.shape[0]
    steps = 2
    tall = rows // steps
    piece = pl.BlockSpec((tall, width), lambda t, m: (t, 0))
    aliased = [] if into is None else [into]
    return pl.pallas_call(
        ortho_kernel,
        out_shape=shape((Y * rows, width), BF16),
        grid_spec=pltpu.PrefetchScalarGridSpec(
            num_scalar_prefetch=1,
            grid=(steps,),
            in_specs=[pl.BlockSpec((k, k), lambda t, m: (0, 0))]
            + [piece] * Y
            + [pl.BlockSpec(memory_space=pl.ANY) for _ in aliased],
            out_specs=pl.BlockSpec((tall, width), lambda t, m: (lax.rem(m[0] + i, Y) * steps + t, 0)),
        ),
        input_output_aliases={} if into is None else {2 + Y: 0},
        compiler_params=pltpu.CompilerParams(vmem_limit_bytes=LIMIT),
        name=f"ortho{i}",
    )(meta, linv, *pieces, *aliased)


def project_kernel(meta, linv, *refs):
    pieces, (out, flat) = refs[: 2 * PARTS], refs[2 * PARTS :]
    k = linv.shape[0]
    width = k // Y
    place(meta, pieces, flat)
    mine = linv[pl.ds(pl.multiple_of(meta[0] * width, width), width), :].astype(F32)
    moment = jnp.concatenate([flat[b * k : (b + 1) * k, :] for b in range(Y)], axis=1)
    half = dot(moment, mine, 1, 1, HI)
    out[...] = dot(linv[...].astype(F32), half, precision=HI)


def project_of(meta, linv, pieces):
    q, width = pieces[0].shape
    k = linv.shape[0]
    return pl.pallas_call(
        project_kernel,
        out_shape=shape((k, width), F32),
        grid_spec=pltpu.PrefetchScalarGridSpec(
            num_scalar_prefetch=1,
            in_specs=[vmem()] * (1 + 2 * PARTS),
            out_specs=vmem(),
            scratch_shapes=[pltpu.VMEM((2 * PARTS * q, width), F32)],
        ),
        compiler_params=pltpu.CompilerParams(vmem_limit_bytes=LIMIT),
        name="project",
    )(meta, linv, *pieces)


def shards(basis, lower, diag, upper, inverse):
    count, size, _ = diag.shape
    r = lax.axis_index("rows")
    c = lax.axis_index("cols")
    meta = jnp.stack([c, lax.rem(r, CORE), r // (Z * CORE), lax.rem(r // CORE, Z)]).astype(jnp.int32)

    rows = X * Z * CORE
    forward = [(i, i + 1) for i in range(rows - 1)]
    low = lax.ppermute(basis[-size:], "rows", forward)
    high = lax.ppermute(basis[:size], "rows", [(b, a) for a, b in forward])

    mats = (lower, diag, upper, inverse)
    work = {j: op_chunk(meta, basis, low, high, *mats, j) for j in (2, 1, 3, 0)}
    piece = {0: dict(work)}
    for s in (2, 1, 3):
        piece[s] = {0: along_cols(work[s], s)}

    wide, top, bottom, keep, send = gram_of(meta, [piece[s][0] for s in range(Y)], size)
    gram = reduce_all(keep, send)
    before = chain(bottom, 1)
    after = chain(top, -1)
    for s in (2, 1, 3):
        for j in range(Y):
            if j != s:
                piece[s][(j - s) % Y] = along_cols(work[j], s)
    keep, send = moment_of(meta, wide, before, after, *mats)
    moment = reduce_all(keep, send)

    linv = factor_of(meta, gram)
    ortho = None
    for i in range(Y):
        ortho = ortho_chunk(meta, linv, [piece[s][i] for s in range(Y)], ortho, i)
    projected = project_of(meta, linv, moment)
    return ortho, projected


def solution(mesh):
    in_specs = (
        P("rows", "cols"),
        P("rows", None, None),
        P("rows", None, None),
        P("rows", None, None),
        P("rows", None, None),
    )
    out_specs = (P("rows", "cols"), P(None, "cols"))
    return jax.shard_map(shards, mesh=mesh, in_specs=in_specs, out_specs=out_specs, check_vma=False)
```

```python
import functools

import jax
import jax.numpy as jnp
from jax import lax
from jax.experimental import pallas as pl
from jax.experimental.pallas import tpu as pltpu
from jax.sharding import PartitionSpec as P

F32 = jnp.float32
BF16 = jnp.bfloat16
HI = lax.Precision.HIGHEST
X, Z, CORE, Y = 4, 4, 2, 4
PARTS = 4
LIMIT = 56 << 20


def dot(a, b, ca=1, cb=0, precision=None):
    return lax.dot_general(
        a, b, (((ca,), (cb,)), ((), ())), precision=precision, preferred_element_type=F32
    )


def cost(flops, bytes_accessed):
    return pl.CostEstimate(flops=flops, transcendentals=0, bytes_accessed=bytes_accessed)


def vmem():
    return pl.BlockSpec(memory_space=pltpu.VMEM)


def shape(dims, dtype):
    return jax.ShapeDtypeStruct(dims, dtype)


def over_rows(move):
    pairs = []
    for x in range(X):
        for z in range(Z):
            for core in range(CORE):
                tx, tz, tc = move(x, z, core)
                source = (x * Z + z) * CORE + core
                pairs.append((source, ((tx % X) * Z + tz % Z) * CORE + tc % CORE))
    return pairs


def flip(value):
    return lax.ppermute(value, "rows", over_rows(lambda x, z, c: (x, z, c + 1)))


PLANE = [[(x * Z + z) * CORE + c for x in range(X) for z in range(Z)] for c in range(CORE)]


def plane(value):
    return lax.all_to_all(value, "rows", 0, 0, tiled=True, axis_index_groups=PLANE)


def along_cols(value, s):
    return lax.ppermute(value, "cols", [(i, (i + s) % Y) for i in range(Y)])


def chain(value, step):
    count = X * Z * CORE * Y
    return lax.ppermute(
        value,
        ("rows", "cols"),
        [(i, i + step) for i in range(count) if 0 <= i + step < count],
    )


def total_of(pieces):
    total = jnp.sum(plane(pieces), axis=0)
    r1, r2, r3 = (along_cols(total, s) for s in (1, 2, 3))
    return (total + r2) + (r1 + r3)


def gathered(piece):
    mine = plane(jnp.broadcast_to(piece[None], (X * Z, *piece.shape)))
    return mine, flip(mine)


def pack_kernel(keep, got, out):
    groups, rows, width = out.shape
    q = rows // Y
    for p in range(groups):
        for d in range(Y):
            at = slice(d * width, (d + 1) * width)
            out[p, d * q : (d + 1) * q, :] = (
                keep[p * q : (p + 1) * q, at] + got[p * q : (p + 1) * q, at]
            )


def pack(keep, got):
    groups = X * Z
    width = keep.shape[1] // Y
    return pl.pallas_call(
        pack_kernel,
        out_shape=shape((groups, keep.shape[0] * Y // groups, width), F32),
        in_specs=[vmem()] * 2,
        out_specs=vmem(),
        cost_estimate=cost(keep.size, 12 * keep.size),
        name="pack",
    )(keep, got)


def apply_blocks(v, lower, diag, upper, inverse, out):
    count, size, _ = diag.shape
    mixed = [
        (dot(lower[k], v[k]) + dot(diag[k], v[k + 1]) + dot(upper[k], v[k + 2])).astype(BF16)
        for k in range(count)
    ]
    for k in range(count):
        out[k * size : (k + 1) * size, :] = dot(inverse[k], mixed[k]).astype(BF16)


def op_kernel(meta, prev, cur, nxt, low, high, lower, diag, upper, inverse, out, *, j, per, count):
    size = diag.shape[1]
    first = lax.rem(meta[0] + j, Y) * (count // Y) + pl.program_id(0) * per
    v = [jnp.where(first == 0, low[...], prev[...])]
    v += [cur[k * size : (k + 1) * size, :] for k in range(per)]
    v += [jnp.where(first + per == count, high[...], nxt[...])]
    apply_blocks(v, lower, diag, upper, inverse, out)


def op_chunk(meta, basis, low, high, lower, diag, upper, inverse, j):
    count, size, _ = diag.shape
    width = basis.shape[1]
    per = 4
    steps = count // Y // per

    def block(i, m):
        return lax.rem(m[0] + j, Y) * steps + i

    def at(i, m):
        return (block(i, m), 0)

    def weights(i, m):
        return (block(i, m), 0, 0)

    mat = pl.BlockSpec((per, size, size), weights)
    return pl.pallas_call(
        functools.partial(op_kernel, j=j, per=per, count=count),
        out_shape=shape((count // Y * size, width), BF16),
        grid_spec=pltpu.PrefetchScalarGridSpec(
            num_scalar_prefetch=1,
            grid=(steps,),
            in_specs=[
                pl.BlockSpec((size, width), lambda i, m: (jnp.maximum(block(i, m) * per - 1, 0), 0)),
                pl.BlockSpec((per * size, width), at),
                pl.BlockSpec(
                    (size, width), lambda i, m: (jnp.minimum(block(i, m) * per + per, count - 1), 0)
                ),
                pl.BlockSpec((size, width), lambda i, m: (0, 0)),
                pl.BlockSpec((size, width), lambda i, m: (0, 0)),
                mat,
                mat,
                mat,
                mat,
            ],
            out_specs=pl.BlockSpec((per * size, width), lambda i, m: (i, 0)),
        ),
        cost_estimate=cost(8 * size * size * width * count // Y, 10 * size * size * count // Y),
        compiler_params=pltpu.CompilerParams(vmem_limit_bytes=LIMIT),
        name=f"op{j}",
    )(meta, basis, basis, basis, low, high, lower, diag, upper, inverse)


def gram_kernel(meta, p0, p1, p2, p3, wide, top, bottom, keep, send, full, flat, *, size):
    width = p0.shape[1]
    for s, piece in enumerate((p0, p1, p2, p3)):
        at = lax.rem(meta[0] + Y - s, Y) * width
        wide[:, pl.ds(pl.multiple_of(at, width), width)] = piece[...]
    rows = wide.shape[0]
    top[...] = wide[0:size, :]
    bottom[...] = wide[rows - size : rows, :]
    full[...] = dot(wide[...], wide[...], 0, 0)
    n = 0
    for a in range(Y):
        for b in range(a, Y):
            flat[n * width : (n + 1) * width, :] = full[
                a * width : (a + 1) * width, b * width : (b + 1) * width
            ]
            n += 1
    half = flat.shape[0] // 2
    core = meta[1]
    keep[...] = flat[pl.ds(pl.multiple_of(core * half, 8), half), :]
    send[...] = flat[pl.ds(pl.multiple_of((1 - core) * half, 8), half), :]


def gram_of(meta, pieces, size):
    rows, width = pieces[0].shape
    k = Y * width
    n = Y * (Y + 1) // 2 * width
    return pl.pallas_call(
        functools.partial(gram_kernel, size=size),
        out_shape=(
            shape((rows, k), BF16),
            shape((size, k), BF16),
            shape((size, k), BF16),
            shape((n // 2, width), F32),
            shape((n // 2, width), F32),
        ),
        grid_spec=pltpu.PrefetchScalarGridSpec(
            num_scalar_prefetch=1,
            in_specs=[vmem()] * 4,
            out_specs=(vmem(),) * 5,
            scratch_shapes=[pltpu.VMEM((k, k), F32), pltpu.VMEM((n, width), F32)],
        ),
        cost_estimate=cost(2 * rows * k * k, 4 * rows * k + 4 * k * k),
        compiler_params=pltpu.CompilerParams(vmem_limit_bytes=LIMIT),
        name="gram",
    )(meta, *pieces)


def moment_kernel(meta, prev, cur, nxt, low, high, lower, diag, upper, inverse, keep, send, acc, image):
    i = pl.program_id(0)
    last = pl.num_programs(0) - 1
    per, size, _ = diag.shape
    v = [jnp.where(i == 0, low[...], prev[...])]
    v += [cur[k * size : (k + 1) * size, :] for k in range(per)]
    v += [jnp.where(i == last, high[...], nxt[...])]
    apply_blocks(v, lower, diag, upper, inverse, image)
    term = dot(cur[...], image[...], 0, 0)

    @pl.when(i == 0)
    def _():
        acc[...] = term

    @pl.when(i > 0)
    def _():
        acc[...] += term

    @pl.when(i == last)
    def _():
        half = acc.shape[0] // 2
        core = meta[1]
        keep[...] = acc[pl.ds(pl.multiple_of(core * half, 8), half), :]
        send[...] = acc[pl.ds(pl.multiple_of((1 - core) * half, 8), half), :]


def moment_of(meta, wide, low, high, lower, diag, upper, inverse):
    count, size, _ = diag.shape
    per = 4
    steps = count // Y // per
    blocks = steps * per
    k = wide.shape[1]
    mat = pl.BlockSpec((per, size, size), lambda i, m: (m[0] * steps + i, 0, 0))
    out = pl.BlockSpec((k // 2, k), lambda i, m: (0, 0))
    return pl.pallas_call(
        moment_kernel,
        out_shape=(shape((k // 2, k), F32), shape((k // 2, k), F32)),
        grid_spec=pltpu.PrefetchScalarGridSpec(
            num_scalar_prefetch=1,
            grid=(steps,),
            in_specs=[
                pl.BlockSpec((size, k), lambda i, m: (jnp.maximum(i * per - 1, 0), 0)),
                pl.BlockSpec((per * size, k), lambda i, m: (i, 0)),
                pl.BlockSpec((size, k), lambda i, m: (jnp.minimum(i * per + per, blocks - 1), 0)),
                pl.BlockSpec((size, k), lambda i, m: (0, 0)),
                pl.BlockSpec((size, k), lambda i, m: (0, 0)),
                mat,
                mat,
                mat,
                mat,
            ],
            out_specs=(out, out),
            scratch_shapes=[pltpu.VMEM((k, k), F32), pltpu.VMEM((per * size, k), BF16)],
        ),
        cost_estimate=cost(blocks * size * k * (8 * size + 2 * k), 4 * blocks * size * k),
        compiler_params=pltpu.CompilerParams(vmem_limit_bytes=LIMIT),
        name="moment",
    )(meta, wide, wide, wide, low, high, lower, diag, upper, inverse)


def eliminate(a):
    groups = len(a)
    wide = (8, 8 * groups)
    sub = lax.broadcasted_iota(jnp.int32, wide, 0)
    lane = lax.broadcasted_iota(jnp.int32, wide, 1)
    a = list(a)

    def column(value, k):
        return jnp.broadcast_to(value[:, k : k + 1], wide)

    def row(value, k):
        return jnp.broadcast_to(value[k : k + 1, :], wide)

    done = []
    for g in range(groups):
        base = 8 * g
        cols = [column(a[g], base + k) for k in range(8)]
        d = [[row(cols[k], i) if i >= k else None for k in range(8)] for i in range(8)]
        low = [[None] * 8 for _ in range(8)]
        scale = [None] * 8
        for k in range(8):
            scale[k] = lax.rsqrt(d[k][k])
            ratio = 1.0 / d[k][k]
            for i in range(k + 1, 8):
                low[i][k] = d[i][k] * scale[k]
                for j in range(k + 1, i + 1):
                    d[i][j] = d[i][j] - (d[i][k] * d[j][k]) * ratio

        def forward(value):
            out = []
            for k in range(8):
                x = value[k]
                for j in range(k):
                    x = x - low[k][j] * out[j]
                out.append(x * scale[k])
            return out

        inside = (lane >= base) & (lane < base + 8)
        own = jnp.where(inside, jnp.where(lane - base == sub, 1.0, 0.0), a[g])
        r = forward([row(own, k) for k in range(8)])
        w = [None] * 8
        if g + 2 < groups:
            for k in reversed(range(8)):
                x = r[k]
                for j in range(k + 1, 8):
                    x = x - low[j][k] * w[j]
                w[k] = x * scale[k]
        for h in range(g + 1, groups):
            c = [column(a[h], base + k) for k in range(8)]
            if h == g + 1:
                c = forward(c)
            x = jnp.where(inside, 0.0, a[h])
            for k in range(8):
                x = x - c[k] * (r if h == g + 1 else w)[k]
            a[h] = x
        rows = r[0]
        for k in range(1, 8):
            rows = jnp.where(sub == k, r[k], rows)
        done.append(jnp.where(lane <= sub + base, rows, 0.0))
    return done


def factor_kernel(meta, mine, other, out, w, inv, flat):
    n = w.shape[0]
    nb = n // Y
    groups = mine.shape[0]
    tall = flat.shape[0] // (2 * groups)
    for which, half in ((mine, meta[1]), (other, 1 - meta[1])):
        for p in range(groups):
            at = pl.multiple_of((half * groups + p) * tall, 8)
            flat[pl.ds(at, tall), :] = which[p, 0:tall, :]
    at = 0
    for a in range(Y):
        for b in range(a, Y):
            block = flat[at : at + nb, :]
            w[a * nb : (a + 1) * nb, b * nb : (b + 1) * nb] = block
            if a != b:
                w[b * nb : (b + 1) * nb, a * nb : (a + 1) * nb] = block.T
            at += nb
    def trail(p, l21, r12):
        lo, hi = p * nb, (p + 1) * nb
        w[hi:n, hi:n] = w[hi:n, hi:n] - dot(l21, r12, precision=HI)
        new = dot(l21, inv[lo:hi, 0:hi], precision=HI)
        if p:
            inv[hi:n, 0:lo] = inv[hi:n, 0:lo] - new[:, 0:lo]
        inv[hi:n, lo:hi] = -new[:, lo:hi]

    diag = w[0:nb, 0:nb]
    held = None
    for p in range(Y):
        lo, hi = p * nb, (p + 1) * nb
        li = jnp.concatenate(
            eliminate([diag[8 * g : 8 * g + 8, :] for g in range(nb // 8)]), axis=0
        )
        if held:
            trail(p - 1, *held)
            inv[lo:hi, 0:lo] = dot(li, inv[lo:hi, 0:lo], precision=HI)
        inv[lo:hi, lo:hi] = li
        if hi < n:
            inv[lo:hi, hi:n] = jnp.zeros((nb, n - hi), F32)
            held = (dot(w[hi:n, lo:hi], li, 1, 1, HI), dot(li, w[lo:hi, hi:n], precision=HI))
            diag = w[hi : hi + nb, hi : hi + nb] - dot(held[0][0:nb], held[1][:, 0:nb], precision=HI)
    out[...] = inv[...].astype(BF16)


def factor_of(meta, mine, other):
    width = mine.shape[2]
    k = Y * width
    return pl.pallas_call(
        factor_kernel,
        out_shape=shape((k, k), BF16),
        grid_spec=pltpu.PrefetchScalarGridSpec(
            num_scalar_prefetch=1,
            in_specs=[vmem()] * 2,
            out_specs=vmem(),
            scratch_shapes=[
                pltpu.VMEM((k, k), F32),
                pltpu.VMEM((k, k), F32),
                pltpu.VMEM((Y * (Y + 1) // 2 * width, width), F32),
            ],
        ),
        cost_estimate=cost(k * k * k, 12 * k * k),
        compiler_params=pltpu.CompilerParams(vmem_limit_bytes=LIMIT),
        name="factor",
    )(meta, mine, other)


def ortho_kernel(meta, linv, wide, *refs):
    outs, full = refs[:Y], refs[Y]
    width = outs[0].shape[1]
    full[...] = dot(wide[...], linv[...], 1, 1).astype(BF16)
    for t in range(Y):
        at = pl.multiple_of(lax.rem(meta[0] + t, Y) * width, width)
        outs[t][...] = full[:, pl.ds(at, width)]


def ortho_of(meta, linv, wide):
    rows, k = wide.shape
    width = k // Y
    return pl.pallas_call(
        ortho_kernel,
        out_shape=[shape((rows, width), BF16)] * Y,
        grid_spec=pltpu.PrefetchScalarGridSpec(
            num_scalar_prefetch=1,
            in_specs=[vmem()] * 2,
            out_specs=[vmem()] * Y,
            scratch_shapes=[pltpu.VMEM((rows, k), BF16)],
        ),
        cost_estimate=cost(2 * rows * k * k, 4 * rows * k),
        compiler_params=pltpu.CompilerParams(vmem_limit_bytes=LIMIT),
        name="ortho",
    )(meta, linv, wide)


def join_kernel(meta, *refs):
    parts, out = refs[:Y], refs[Y]
    rows = parts[0].shape[0]
    for t in range(Y):
        at = pl.multiple_of(lax.rem(meta[0] + Y - t, Y) * rows, rows)
        out[pl.ds(at, rows), :] = parts[t][...]


def join(meta, parts):
    rows, width = parts[0].shape
    return pl.pallas_call(
        join_kernel,
        out_shape=shape((Y * rows, width), BF16),
        grid_spec=pltpu.PrefetchScalarGridSpec(
            num_scalar_prefetch=1, in_specs=[vmem()] * Y, out_specs=vmem()
        ),
        cost_estimate=cost(0, 4 * Y * rows * width),
        compiler_params=pltpu.CompilerParams(vmem_limit_bytes=LIMIT),
        name="join",
    )(meta, *parts)


def thirds(x):
    a = x.astype(BF16)
    x = x - a.astype(F32)
    b = x.astype(BF16)
    return a, b, (x - b.astype(F32)).astype(BF16)


def tail_kernel(meta, linv, moment, out):
    q, width = out.shape
    rows = linv[pl.ds(pl.multiple_of(meta[0] * width, width), width), :]
    out[...] = sum(
        dot(part, rows[:, d * width : (d + 1) * width], 1, 1)
        for d in range(Y)
        for part in thirds(moment[d * q : (d + 1) * q, :])
    )


def tail_of(meta, linv, moment):
    rows, width = moment.shape
    return pl.pallas_call(
        tail_kernel,
        out_shape=shape((rows // Y, width), F32),
        grid_spec=pltpu.PrefetchScalarGridSpec(
            num_scalar_prefetch=1, in_specs=[vmem()] * 2, out_specs=vmem()
        ),
        cost_estimate=cost(6 * rows * width * width, 2 * linv.size),
        name="tail",
    )(meta, linv, moment)


def project_kernel(meta, linv, mine, other, out, full):
    groups, q, _ = mine.shape
    for which, half in ((mine, meta[1]), (other, 1 - meta[1])):
        for p in range(groups):
            full[pl.ds(pl.multiple_of((half * groups + p) * q, q), q), :] = which[p]
    out[...] = sum(dot(linv[...], part) for part in thirds(full[...]))


def project_of(meta, linv, mine, other):
    k = linv.shape[0]
    width = k // Y
    return pl.pallas_call(
        project_kernel,
        out_shape=shape((k, width), F32),
        grid_spec=pltpu.PrefetchScalarGridSpec(
            num_scalar_prefetch=1,
            in_specs=[vmem()] * 3,
            out_specs=vmem(),
            scratch_shapes=[pltpu.VMEM((k, width), F32)],
        ),
        cost_estimate=cost(6 * k * k * width, 4 * k * k),
        name="project",
    )(meta, linv, mine, other)


def shards(basis, lower, diag, upper, inverse):
    count, size, _ = diag.shape
    r = lax.axis_index("rows")
    c = lax.axis_index("cols")
    meta = jnp.stack([c, lax.rem(r, CORE)]).astype(jnp.int32)

    rows = X * Z * CORE
    forward = [(i, i + 1) for i in range(rows - 1)]
    low = lax.ppermute(basis[-size:], "rows", forward)
    high = lax.ppermute(basis[:size], "rows", [(b, a) for a, b in forward])

    mats = (lower, diag, upper, inverse)
    work = {j: op_chunk(meta, basis, low, high, *mats, j) for j in (2, 1, 3, 0)}
    near = [work[0]] + [along_cols(work[s], s) for s in (1, 2, 3)]
    wide, top, bottom, keep, send = gram_of(meta, near, size)

    half = keep + flip(send)
    gram = total_of(half.reshape(X * Z, -1, half.shape[1]))
    linv = factor_of(meta, *gathered(gram))
    parts = ortho_of(meta, linv, wide)
    ortho = join(meta, [parts[0]] + [along_cols(parts[t], t) for t in (1, 2, 3)])

    before = chain(bottom, 1)
    after = chain(top, -1)
    keep, send = moment_of(meta, wide, before, after, *mats)
    moment = total_of(pack(keep, flip(send)))
    projected = project_of(meta, linv, *gathered(tail_of(meta, linv, moment)))
    return ortho, projected


def solution(mesh):
    in_specs = (
        P("rows", "cols"),
        P("rows", None, None),
        P("rows", None, None),
        P("rows", None, None),
        P("rows", None, None),
    )
    out_specs = (P("rows", "cols"), P(None, "cols"))
    return jax.shard_map(shards, mesh=mesh, in_specs=in_specs, out_specs=out_specs, check_vma=False)
```

```python
import functools

import jax
import jax.numpy as jnp
from jax import lax
from jax.experimental import pallas as pl
from jax.experimental.pallas import tpu as pltpu
from jax.sharding import PartitionSpec as P

F32 = jnp.float32
BF16 = jnp.bfloat16
HI = lax.Precision.HIGHEST
X, Z, CORE, Y = 4, 4, 2, 4
PARTS = 4
LIMIT = 24 << 20
WHOLE = 56 << 20


def dot(a, b, ca=1, cb=0, precision=None):
    return lax.dot_general(
        a, b, (((ca,), (cb,)), ((), ())), precision=precision, preferred_element_type=F32
    )


def cost(flops, bytes_accessed):
    return pl.CostEstimate(flops=flops, transcendentals=0, bytes_accessed=bytes_accessed)


def vmem():
    return pl.BlockSpec(memory_space=pltpu.VMEM)


def shape(dims, dtype):
    return jax.ShapeDtypeStruct(dims, dtype)


def over_rows(move):
    pairs = []
    for x in range(X):
        for z in range(Z):
            for core in range(CORE):
                tx, tz, tc = move(x, z, core)
                source = (x * Z + z) * CORE + core
                pairs.append((source, ((tx % X) * Z + tz % Z) * CORE + tc % CORE))
    return pairs


def flip(value):
    return lax.ppermute(value, "rows", over_rows(lambda x, z, c: (x, z, c + 1)))


PLANE = [[(x * Z + z) * CORE + c for x in range(X) for z in range(Z)] for c in range(CORE)]


def plane(value):
    return lax.all_to_all(value, "rows", 0, 0, tiled=True, axis_index_groups=PLANE)


def along_cols(value, s):
    return lax.ppermute(value, "cols", [(i, (i + s) % Y) for i in range(Y)])


def chain(value, step):
    count = X * Z * CORE * Y
    return lax.ppermute(
        value,
        ("rows", "cols"),
        [(i, i + step) for i in range(count) if 0 <= i + step < count],
    )


def total_of(pieces):
    total = jnp.sum(plane(pieces), axis=0)
    r1, r2, r3 = (along_cols(total, s) for s in (1, 2, 3))
    return (total + r2) + (r1 + r3)


def gathered(piece):
    mine = plane(jnp.broadcast_to(piece[None], (X * Z, *piece.shape)))
    return mine, flip(mine)


def pack_kernel(keep, got, out):
    groups, rows, width = out.shape
    q = rows // Y
    for p in range(groups):
        for d in range(Y):
            at = slice(d * width, (d + 1) * width)
            out[p, d * q : (d + 1) * q, :] = (
                keep[p * q : (p + 1) * q, at] + got[p * q : (p + 1) * q, at]
            )


def pack(keep, got):
    groups = X * Z
    width = keep.shape[1] // Y
    return pl.pallas_call(
        pack_kernel,
        out_shape=shape((groups, keep.shape[0] * Y // groups, width), F32),
        in_specs=[vmem()] * 2,
        out_specs=vmem(),
        cost_estimate=cost(keep.size, 12 * keep.size),
        name="pack",
    )(keep, got)


def apply_blocks(v, lower, diag, upper, inverse, out):
    count, size, _ = diag.shape
    mixed = [
        (dot(lower[k], v[k]) + dot(diag[k], v[k + 1]) + dot(upper[k], v[k + 2])).astype(BF16)
        for k in range(count)
    ]
    for k in range(count):
        out[k * size : (k + 1) * size, :] = dot(inverse[k], mixed[k]).astype(BF16)


def op_kernel(meta, prev, cur, nxt, low, high, lower, diag, upper, inverse, out, *, j, per, count):
    size = diag.shape[1]
    first = lax.rem(meta[0] + j, Y) * (count // Y) + pl.program_id(0) * per
    v = [jnp.where(first == 0, low[...], prev[...])]
    v += [cur[k * size : (k + 1) * size, :] for k in range(per)]
    v += [jnp.where(first + per == count, high[...], nxt[...])]
    apply_blocks(v, lower, diag, upper, inverse, out)


def op_chunk(meta, basis, low, high, lower, diag, upper, inverse, j):
    count, size, _ = diag.shape
    width = basis.shape[1]
    per = 4
    steps = count // Y // per

    def block(i, m):
        return lax.rem(m[0] + j, Y) * steps + i

    def at(i, m):
        return (block(i, m), 0)

    def weights(i, m):
        return (block(i, m), 0, 0)

    mat = pl.BlockSpec((per, size, size), weights)
    return pl.pallas_call(
        functools.partial(op_kernel, j=j, per=per, count=count),
        out_shape=shape((count // Y * size, width), BF16),
        grid_spec=pltpu.PrefetchScalarGridSpec(
            num_scalar_prefetch=1,
            grid=(steps,),
            in_specs=[
                pl.BlockSpec((size, width), lambda i, m: (jnp.maximum(block(i, m) * per - 1, 0), 0)),
                pl.BlockSpec((per * size, width), at),
                pl.BlockSpec(
                    (size, width), lambda i, m: (jnp.minimum(block(i, m) * per + per, count - 1), 0)
                ),
                pl.BlockSpec((size, width), lambda i, m: (0, 0)),
                pl.BlockSpec((size, width), lambda i, m: (0, 0)),
                mat,
                mat,
                mat,
                mat,
            ],
            out_specs=pl.BlockSpec((per * size, width), lambda i, m: (i, 0)),
        ),
        cost_estimate=cost(8 * size * size * width * count // Y, 10 * size * size * count // Y),
        compiler_params=pltpu.CompilerParams(vmem_limit_bytes=WHOLE),
        name=f"op{j}",
    )(meta, basis, basis, basis, low, high, lower, diag, upper, inverse)


def gram_kernel(meta, p0, p1, p2, p3, wide, top, bottom, keep, send, full, flat, *, size):
    width = p0.shape[1]
    for s, piece in enumerate((p0, p1, p2, p3)):
        at = lax.rem(meta[0] + Y - s, Y) * width
        wide[:, pl.ds(pl.multiple_of(at, width), width)] = piece[...]
    rows = wide.shape[0]
    top[...] = wide[0:size, :]
    bottom[...] = wide[rows - size : rows, :]
    full[...] = dot(wide[...], wide[...], 0, 0)
    n = 0
    for a in range(Y):
        for b in range(a, Y):
            flat[n * width : (n + 1) * width, :] = full[
                a * width : (a + 1) * width, b * width : (b + 1) * width
            ]
            n += 1
    half = flat.shape[0] // 2
    core = meta[1]
    keep[...] = flat[pl.ds(pl.multiple_of(core * half, 8), half), :]
    send[...] = flat[pl.ds(pl.multiple_of((1 - core) * half, 8), half), :]


def gram_of(meta, pieces, size):
    rows, width = pieces[0].shape
    k = Y * width
    n = Y * (Y + 1) // 2 * width
    return pl.pallas_call(
        functools.partial(gram_kernel, size=size),
        out_shape=(
            shape((rows, k), BF16),
            shape((size, k), BF16),
            shape((size, k), BF16),
            shape((n // 2, width), F32),
            shape((n // 2, width), F32),
        ),
        grid_spec=pltpu.PrefetchScalarGridSpec(
            num_scalar_prefetch=1,
            in_specs=[vmem()] * 4,
            out_specs=(vmem(),) * 5,
            scratch_shapes=[pltpu.VMEM((k, k), F32), pltpu.VMEM((n, width), F32)],
        ),
        cost_estimate=cost(2 * rows * k * k, 4 * rows * k + 4 * k * k),
        compiler_params=pltpu.CompilerParams(vmem_limit_bytes=LIMIT),
        name="gram",
    )(meta, *pieces)


def moment_kernel(meta, prev, cur, nxt, low, high, lower, diag, upper, inverse, keep, send, acc, image):
    i = pl.program_id(0)
    last = pl.num_programs(0) - 1
    per, size, _ = diag.shape
    v = [jnp.where(i == 0, low[...], prev[...])]
    v += [cur[k * size : (k + 1) * size, :] for k in range(per)]
    v += [jnp.where(i == last, high[...], nxt[...])]
    apply_blocks(v, lower, diag, upper, inverse, image)
    term = dot(cur[...], image[...], 0, 0)

    @pl.when(i == 0)
    def _():
        acc[...] = term

    @pl.when(i > 0)
    def _():
        acc[...] += term

    @pl.when(i == last)
    def _():
        half = acc.shape[0] // 2
        core = meta[1]
        keep[...] = acc[pl.ds(pl.multiple_of(core * half, 8), half), :]
        send[...] = acc[pl.ds(pl.multiple_of((1 - core) * half, 8), half), :]


def moment_of(meta, wide, low, high, lower, diag, upper, inverse):
    count, size, _ = diag.shape
    per = 4
    steps = count // Y // per
    blocks = steps * per
    k = wide.shape[1]
    mat = pl.BlockSpec((per, size, size), lambda i, m: (m[0] * steps + i, 0, 0))
    out = pl.BlockSpec((k // 2, k), lambda i, m: (0, 0))
    return pl.pallas_call(
        moment_kernel,
        out_shape=(shape((k // 2, k), F32), shape((k // 2, k), F32)),
        grid_spec=pltpu.PrefetchScalarGridSpec(
            num_scalar_prefetch=1,
            grid=(steps,),
            in_specs=[
                pl.BlockSpec((size, k), lambda i, m: (jnp.maximum(i * per - 1, 0), 0)),
                pl.BlockSpec((per * size, k), lambda i, m: (i, 0)),
                pl.BlockSpec((size, k), lambda i, m: (jnp.minimum(i * per + per, blocks - 1), 0)),
                pl.BlockSpec((size, k), lambda i, m: (0, 0)),
                pl.BlockSpec((size, k), lambda i, m: (0, 0)),
                mat,
                mat,
                mat,
                mat,
            ],
            out_specs=(out, out),
            scratch_shapes=[pltpu.VMEM((k, k), F32), pltpu.VMEM((per * size, k), BF16)],
        ),
        cost_estimate=cost(blocks * size * k * (8 * size + 2 * k), 4 * blocks * size * k),
        compiler_params=pltpu.CompilerParams(vmem_limit_bytes=WHOLE),
        name="moment",
    )(meta, wide, wide, wide, low, high, lower, diag, upper, inverse)


def eliminate(a):
    groups = len(a)
    wide = (8, 8 * groups)
    sub = lax.broadcasted_iota(jnp.int32, wide, 0)
    lane = lax.broadcasted_iota(jnp.int32, wide, 1)
    a = list(a)

    def column(value, k):
        return jnp.broadcast_to(value[:, k : k + 1], wide)

    def row(value, k):
        return jnp.broadcast_to(value[k : k + 1, :], wide)

    done = []
    for g in range(groups):
        base = 8 * g
        cols = [column(a[g], base + k) for k in range(8)]
        d = [[row(cols[k], i) if i >= k else None for k in range(8)] for i in range(8)]
        low = [[None] * 8 for _ in range(8)]
        scale = [None] * 8
        for k in range(8):
            scale[k] = lax.rsqrt(d[k][k])
            ratio = 1.0 / d[k][k]
            for i in range(k + 1, 8):
                low[i][k] = d[i][k] * scale[k]
                for j in range(k + 1, i + 1):
                    d[i][j] = d[i][j] - (d[i][k] * d[j][k]) * ratio

        def forward(value):
            out = []
            for k in range(8):
                x = value[k]
                for j in range(k):
                    x = x - low[k][j] * out[j]
                out.append(x * scale[k])
            return out

        inside = (lane >= base) & (lane < base + 8)
        own = jnp.where(inside, jnp.where(lane - base == sub, 1.0, 0.0), a[g])
        r = forward([row(own, k) for k in range(8)])
        w = [None] * 8
        if g + 2 < groups:
            for k in reversed(range(8)):
                x = r[k]
                for j in range(k + 1, 8):
                    x = x - low[j][k] * w[j]
                w[k] = x * scale[k]
        for h in range(g + 1, groups):
            c = [column(a[h], base + k) for k in range(8)]
            if h == g + 1:
                c = forward(c)
            x = jnp.where(inside, 0.0, a[h])
            for k in range(8):
                x = x - c[k] * (r if h == g + 1 else w)[k]
            a[h] = x
        rows = r[0]
        for k in range(1, 8):
            rows = jnp.where(sub == k, r[k], rows)
        done.append(jnp.where(lane <= sub + base, rows, 0.0))
    return done


def factor_kernel(meta, mine, other, out, w, inv, flat):
    n = w.shape[0]
    nb = n // Y
    groups = mine.shape[0]
    tall = flat.shape[0] // (2 * groups)
    for which, half in ((mine, meta[1]), (other, 1 - meta[1])):
        for p in range(groups):
            at = pl.multiple_of((half * groups + p) * tall, 8)
            flat[pl.ds(at, tall), :] = which[p, 0:tall, :]
    at = 0
    for a in range(Y):
        for b in range(a, Y):
            block = flat[at : at + nb, :]
            w[a * nb : (a + 1) * nb, b * nb : (b + 1) * nb] = block
            if a != b:
                w[b * nb : (b + 1) * nb, a * nb : (a + 1) * nb] = block.T
            at += nb
    def trail(p, l21, r12):
        lo, hi = p * nb, (p + 1) * nb
        w[hi:n, hi:n] = w[hi:n, hi:n] - dot(l21, r12, precision=HI)
        new = dot(l21, inv[lo:hi, 0:hi], precision=HI)
        if p:
            inv[hi:n, 0:lo] = inv[hi:n, 0:lo] - new[:, 0:lo]
        inv[hi:n, lo:hi] = -new[:, lo:hi]

    diag = w[0:nb, 0:nb]
    held = None
    for p in range(Y):
        lo, hi = p * nb, (p + 1) * nb
        li = jnp.concatenate(
            eliminate([diag[8 * g : 8 * g + 8, :] for g in range(nb // 8)]), axis=0
        )
        if held:
            trail(p - 1, *held)
            inv[lo:hi, 0:lo] = dot(li, inv[lo:hi, 0:lo], precision=HI)
        inv[lo:hi, lo:hi] = li
        if hi < n:
            inv[lo:hi, hi:n] = jnp.zeros((nb, n - hi), F32)
            held = (dot(w[hi:n, lo:hi], li, 1, 1, HI), dot(li, w[lo:hi, hi:n], precision=HI))
            diag = w[hi : hi + nb, hi : hi + nb] - dot(held[0][0:nb], held[1][:, 0:nb], precision=HI)
    out[...] = inv[...].astype(BF16)


def factor_of(meta, mine, other):
    width = mine.shape[2]
    k = Y * width
    return pl.pallas_call(
        factor_kernel,
        out_shape=shape((k, k), BF16),
        grid_spec=pltpu.PrefetchScalarGridSpec(
            num_scalar_prefetch=1,
            in_specs=[vmem()] * 2,
            out_specs=vmem(),
            scratch_shapes=[
                pltpu.VMEM((k, k), F32),
                pltpu.VMEM((k, k), F32),
                pltpu.VMEM((Y * (Y + 1) // 2 * width, width), F32),
            ],
        ),
        cost_estimate=cost(k * k * k, 12 * k * k),
        compiler_params=pltpu.CompilerParams(vmem_limit_bytes=LIMIT),
        name="factor",
    )(meta, mine, other)


def ortho_kernel(meta, linv, wide, *refs):
    outs, full = refs[:Y], refs[Y]
    width = outs[0].shape[1]
    full[...] = dot(wide[...], linv[...], 1, 1).astype(BF16)
    for t in range(Y):
        at = pl.multiple_of(lax.rem(meta[0] + t, Y) * width, width)
        outs[t][...] = full[:, pl.ds(at, width)]


def ortho_of(meta, linv, wide):
    rows, k = wide.shape
    width = k // Y
    return pl.pallas_call(
        ortho_kernel,
        out_shape=[shape((rows, width), BF16)] * Y,
        grid_spec=pltpu.PrefetchScalarGridSpec(
            num_scalar_prefetch=1,
            in_specs=[vmem()] * 2,
            out_specs=[vmem()] * Y,
            scratch_shapes=[pltpu.VMEM((rows, k), BF16)],
        ),
        cost_estimate=cost(2 * rows * k * k, 4 * rows * k),
        compiler_params=pltpu.CompilerParams(vmem_limit_bytes=LIMIT),
        name="ortho",
    )(meta, linv, wide)


def join_kernel(meta, *refs):
    parts, out = refs[:Y], refs[Y]
    rows = parts[0].shape[0]
    for t in range(Y):
        at = pl.multiple_of(lax.rem(meta[0] + Y - t, Y) * rows, rows)
        out[pl.ds(at, rows), :] = parts[t][...]


def join(meta, parts):
    rows, width = parts[0].shape
    return pl.pallas_call(
        join_kernel,
        out_shape=shape((Y * rows, width), BF16),
        grid_spec=pltpu.PrefetchScalarGridSpec(
            num_scalar_prefetch=1, in_specs=[vmem()] * Y, out_specs=vmem()
        ),
        cost_estimate=cost(0, 4 * Y * rows * width),
        compiler_params=pltpu.CompilerParams(vmem_limit_bytes=LIMIT),
        name="join",
    )(meta, *parts)


def thirds(x):
    a = x.astype(BF16)
    x = x - a.astype(F32)
    b = x.astype(BF16)
    return a, b, (x - b.astype(F32)).astype(BF16)


def tail_kernel(meta, linv, moment, out):
    q, width = out.shape
    rows = linv[pl.ds(pl.multiple_of(meta[0] * width, width), width), :]
    out[...] = sum(
        dot(part, rows[:, d * width : (d + 1) * width], 1, 1)
        for d in range(Y)
        for part in thirds(moment[d * q : (d + 1) * q, :])
    )


def tail_of(meta, linv, moment):
    rows, width = moment.shape
    return pl.pallas_call(
        tail_kernel,
        out_shape=shape((rows // Y, width), F32),
        grid_spec=pltpu.PrefetchScalarGridSpec(
            num_scalar_prefetch=1, in_specs=[vmem()] * 2, out_specs=vmem()
        ),
        cost_estimate=cost(6 * rows * width * width, 2 * linv.size),
        name="tail",
    )(meta, linv, moment)


def project_kernel(meta, linv, mine, other, out, full):
    groups, q, _ = mine.shape
    for which, half in ((mine, meta[1]), (other, 1 - meta[1])):
        for p in range(groups):
            full[pl.ds(pl.multiple_of((half * groups + p) * q, q), q), :] = which[p]
    out[...] = sum(dot(linv[...], part) for part in thirds(full[...]))


def project_of(meta, linv, mine, other):
    k = linv.shape[0]
    width = k // Y
    return pl.pallas_call(
        project_kernel,
        out_shape=shape((k, width), F32),
        grid_spec=pltpu.PrefetchScalarGridSpec(
            num_scalar_prefetch=1,
            in_specs=[vmem()] * 3,
            out_specs=vmem(),
            scratch_shapes=[pltpu.VMEM((k, width), F32)],
        ),
        cost_estimate=cost(6 * k * k * width, 4 * k * k),
        name="project",
    )(meta, linv, mine, other)


def shards(basis, lower, diag, upper, inverse):
    count, size, _ = diag.shape
    r = lax.axis_index("rows")
    c = lax.axis_index("cols")
    meta = jnp.stack([c, lax.rem(r, CORE)]).astype(jnp.int32)

    rows = X * Z * CORE
    forward = [(i, i + 1) for i in range(rows - 1)]
    low = lax.ppermute(basis[-size:], "rows", forward)
    high = lax.ppermute(basis[:size], "rows", [(b, a) for a, b in forward])

    mats = (lower, diag, upper, inverse)
    work = {j: op_chunk(meta, basis, low, high, *mats, j) for j in (2, 1, 3, 0)}
    near = [work[0]] + [along_cols(work[s], s) for s in (1, 2, 3)]
    wide, top, bottom, keep, send = gram_of(meta, near, size)

    half = keep + flip(send)
    gram = total_of(half.reshape(X * Z, -1, half.shape[1]))
    linv = factor_of(meta, *gathered(gram))
    parts = ortho_of(meta, linv, wide)
    ortho = join(meta, [parts[0]] + [along_cols(parts[t], t) for t in (1, 2, 3)])

    before = chain(bottom, 1)
    after = chain(top, -1)
    keep, send = moment_of(meta, wide, before, after, *mats)
    moment = total_of(pack(keep, flip(send)))
    projected = project_of(meta, linv, *gathered(tail_of(meta, linv, moment)))
    return ortho, projected


def solution(mesh):
    in_specs = (
        P("rows", "cols"),
        P("rows", None, None),
        P("rows", None, None),
        P("rows", None, None),
        P("rows", None, None),
    )
    out_specs = (P("rows", "cols"), P(None, "cols"))
    return jax.shard_map(shards, mesh=mesh, in_specs=in_specs, out_specs=out_specs, check_vma=False)
```

```python
import functools

import jax
import jax.numpy as jnp
from jax import lax
from jax.experimental import pallas as pl
from jax.experimental.pallas import tpu as pltpu
from jax.sharding import PartitionSpec as P

F32 = jnp.float32
BF16 = jnp.bfloat16
HI = lax.Precision.HIGHEST
X, Z, CORE, Y = 4, 4, 2, 4
PARTS = 4
LIMIT = 24 << 20
WHOLE = 56 << 20


def dot(a, b, ca=1, cb=0, precision=None):
    return lax.dot_general(
        a, b, (((ca,), (cb,)), ((), ())), precision=precision, preferred_element_type=F32
    )


def cost(flops, bytes_accessed):
    return pl.CostEstimate(flops=flops, transcendentals=0, bytes_accessed=bytes_accessed)


def vmem():
    return pl.BlockSpec(memory_space=pltpu.VMEM)


def shape(dims, dtype):
    return jax.ShapeDtypeStruct(dims, dtype)


def over_rows(move):
    pairs = []
    for x in range(X):
        for z in range(Z):
            for core in range(CORE):
                tx, tz, tc = move(x, z, core)
                source = (x * Z + z) * CORE + core
                pairs.append((source, ((tx % X) * Z + tz % Z) * CORE + tc % CORE))
    return pairs


def flip(value):
    return lax.ppermute(value, "rows", over_rows(lambda x, z, c: (x, z, c + 1)))


PLANE = [[(x * Z + z) * CORE + c for x in range(X) for z in range(Z)] for c in range(CORE)]


def plane(value):
    return lax.all_to_all(value, "rows", 0, 0, tiled=True, axis_index_groups=PLANE)


def along_cols(value, s):
    return lax.ppermute(value, "cols", [(i, (i + s) % Y) for i in range(Y)])


def chain(value, step):
    count = X * Z * CORE * Y
    return lax.ppermute(
        value,
        ("rows", "cols"),
        [(i, i + step) for i in range(count) if 0 <= i + step < count],
    )


def total_of(pieces):
    total = jnp.sum(plane(pieces).astype(F32), axis=0)
    r1, r2, r3 = (along_cols(total, s) for s in (1, 2, 3))
    return (total + r2) + (r1 + r3)


def gathered(piece):
    mine = plane(jnp.broadcast_to(piece[None], (X * Z, *piece.shape)))
    return mine, flip(mine)


def pack_kernel(keep, got, out):
    groups, rows, width = out.shape
    q = rows // Y
    for p in range(groups):
        for d in range(Y):
            at = slice(d * width, (d + 1) * width)
            out[p, d * q : (d + 1) * q, :] = (
                keep[p * q : (p + 1) * q, at] + got[p * q : (p + 1) * q, at]
            ).astype(out.dtype)


def pack(keep, got):
    groups = X * Z
    width = keep.shape[1] // Y
    return pl.pallas_call(
        pack_kernel,
        out_shape=shape((groups, keep.shape[0] * Y // groups, width), BF16),
        in_specs=[vmem()] * 2,
        out_specs=vmem(),
        cost_estimate=cost(keep.size, 12 * keep.size),
        name="pack",
    )(keep, got)


def apply_blocks(v, lower, diag, upper, inverse, out):
    count, size, _ = diag.shape
    mixed = [
        (dot(lower[k], v[k]) + dot(diag[k], v[k + 1]) + dot(upper[k], v[k + 2])).astype(BF16)
        for k in range(count)
    ]
    for k in range(count):
        out[k * size : (k + 1) * size, :] = dot(inverse[k], mixed[k]).astype(BF16)


def op_kernel(meta, prev, cur, nxt, low, high, lower, diag, upper, inverse, out, *, j, per, count):
    size = diag.shape[1]
    first = lax.rem(meta[0] + j, Y) * (count // Y) + pl.program_id(0) * per
    v = [jnp.where(first == 0, low[...], prev[...])]
    v += [cur[k * size : (k + 1) * size, :] for k in range(per)]
    v += [jnp.where(first + per == count, high[...], nxt[...])]
    apply_blocks(v, lower, diag, upper, inverse, out)


def op_chunk(meta, basis, low, high, lower, diag, upper, inverse, j):
    count, size, _ = diag.shape
    width = basis.shape[1]
    per = 4
    steps = count // Y // per

    def block(i, m):
        return lax.rem(m[0] + j, Y) * steps + i

    def at(i, m):
        return (block(i, m), 0)

    def weights(i, m):
        return (block(i, m), 0, 0)

    mat = pl.BlockSpec((per, size, size), weights)
    return pl.pallas_call(
        functools.partial(op_kernel, j=j, per=per, count=count),
        out_shape=shape((count // Y * size, width), BF16),
        grid_spec=pltpu.PrefetchScalarGridSpec(
            num_scalar_prefetch=1,
            grid=(steps,),
            in_specs=[
                pl.BlockSpec((size, width), lambda i, m: (jnp.maximum(block(i, m) * per - 1, 0), 0)),
                pl.BlockSpec((per * size, width), at),
                pl.BlockSpec(
                    (size, width), lambda i, m: (jnp.minimum(block(i, m) * per + per, count - 1), 0)
                ),
                pl.BlockSpec((size, width), lambda i, m: (0, 0)),
                pl.BlockSpec((size, width), lambda i, m: (0, 0)),
                mat,
                mat,
                mat,
                mat,
            ],
            out_specs=pl.BlockSpec((per * size, width), lambda i, m: (i, 0)),
        ),
        cost_estimate=cost(8 * size * size * width * count // Y, 10 * size * size * count // Y),
        compiler_params=pltpu.CompilerParams(vmem_limit_bytes=WHOLE),
        name=f"op{j}",
    )(meta, basis, basis, basis, low, high, lower, diag, upper, inverse)


def gram_kernel(meta, p0, p1, p2, p3, wide, top, bottom, keep, send, full, flat, *, size):
    width = p0.shape[1]
    for s, piece in enumerate((p0, p1, p2, p3)):
        at = lax.rem(meta[0] + Y - s, Y) * width
        wide[:, pl.ds(pl.multiple_of(at, width), width)] = piece[...]
    rows = wide.shape[0]
    top[...] = wide[0:size, :]
    bottom[...] = wide[rows - size : rows, :]
    full[...] = dot(wide[...], wide[...], 0, 0)
    n = 0
    for a in range(Y):
        for b in range(a, Y):
            flat[n * width : (n + 1) * width, :] = full[
                a * width : (a + 1) * width, b * width : (b + 1) * width
            ]
            n += 1
    half = flat.shape[0] // 2
    core = meta[1]
    keep[...] = flat[pl.ds(pl.multiple_of(core * half, 8), half), :]
    send[...] = flat[pl.ds(pl.multiple_of((1 - core) * half, 8), half), :]


def gram_of(meta, pieces, size):
    rows, width = pieces[0].shape
    k = Y * width
    n = Y * (Y + 1) // 2 * width
    return pl.pallas_call(
        functools.partial(gram_kernel, size=size),
        out_shape=(
            shape((rows, k), BF16),
            shape((size, k), BF16),
            shape((size, k), BF16),
            shape((n // 2, width), F32),
            shape((n // 2, width), F32),
        ),
        grid_spec=pltpu.PrefetchScalarGridSpec(
            num_scalar_prefetch=1,
            in_specs=[vmem()] * 4,
            out_specs=(vmem(),) * 5,
            scratch_shapes=[pltpu.VMEM((k, k), F32), pltpu.VMEM((n, width), F32)],
        ),
        cost_estimate=cost(2 * rows * k * k, 4 * rows * k + 4 * k * k),
        compiler_params=pltpu.CompilerParams(vmem_limit_bytes=LIMIT),
        name="gram",
    )(meta, *pieces)


def moment_kernel(meta, prev, cur, nxt, low, high, lower, diag, upper, inverse, keep, send, acc, image):
    i = pl.program_id(0)
    last = pl.num_programs(0) - 1
    per, size, _ = diag.shape
    v = [jnp.where(i == 0, low[...], prev[...])]
    v += [cur[k * size : (k + 1) * size, :] for k in range(per)]
    v += [jnp.where(i == last, high[...], nxt[...])]
    apply_blocks(v, lower, diag, upper, inverse, image)
    term = dot(cur[...], image[...], 0, 0)

    @pl.when(i == 0)
    def _():
        acc[...] = term

    @pl.when(i > 0)
    def _():
        acc[...] += term

    @pl.when(i == last)
    def _():
        half = acc.shape[0] // 2
        core = meta[1]
        keep[...] = acc[pl.ds(pl.multiple_of(core * half, 8), half), :]
        send[...] = acc[pl.ds(pl.multiple_of((1 - core) * half, 8), half), :]


def moment_of(meta, wide, low, high, lower, diag, upper, inverse):
    count, size, _ = diag.shape
    per = 4
    steps = count // Y // per
    blocks = steps * per
    k = wide.shape[1]
    mat = pl.BlockSpec((per, size, size), lambda i, m: (m[0] * steps + i, 0, 0))
    out = pl.BlockSpec((k // 2, k), lambda i, m: (0, 0))
    return pl.pallas_call(
        moment_kernel,
        out_shape=(shape((k // 2, k), F32), shape((k // 2, k), F32)),
        grid_spec=pltpu.PrefetchScalarGridSpec(
            num_scalar_prefetch=1,
            grid=(steps,),
            in_specs=[
                pl.BlockSpec((size, k), lambda i, m: (jnp.maximum(i * per - 1, 0), 0)),
                pl.BlockSpec((per * size, k), lambda i, m: (i, 0)),
                pl.BlockSpec((size, k), lambda i, m: (jnp.minimum(i * per + per, blocks - 1), 0)),
                pl.BlockSpec((size, k), lambda i, m: (0, 0)),
                pl.BlockSpec((size, k), lambda i, m: (0, 0)),
                mat,
                mat,
                mat,
                mat,
            ],
            out_specs=(out, out),
            scratch_shapes=[pltpu.VMEM((k, k), F32), pltpu.VMEM((per * size, k), BF16)],
        ),
        cost_estimate=cost(blocks * size * k * (8 * size + 2 * k), 4 * blocks * size * k),
        compiler_params=pltpu.CompilerParams(vmem_limit_bytes=WHOLE),
        name="moment",
    )(meta, wide, wide, wide, low, high, lower, diag, upper, inverse)


def eliminate(a):
    groups = len(a)
    wide = (8, 8 * groups)
    sub = lax.broadcasted_iota(jnp.int32, wide, 0)
    lane = lax.broadcasted_iota(jnp.int32, wide, 1)
    a = list(a)

    def column(value, k):
        return jnp.broadcast_to(value[:, k : k + 1], wide)

    def row(value, k):
        return jnp.broadcast_to(value[k : k + 1, :], wide)

    done = []
    for g in range(groups):
        base = 8 * g
        cols = [column(a[g], base + k) for k in range(8)]
        d = [[row(cols[k], i) if i >= k else None for k in range(8)] for i in range(8)]
        low = [[None] * 8 for _ in range(8)]
        scale = [None] * 8
        for k in range(8):
            scale[k] = lax.rsqrt(d[k][k])
            ratio = 1.0 / d[k][k]
            for i in range(k + 1, 8):
                low[i][k] = d[i][k] * scale[k]
                for j in range(k + 1, i + 1):
                    d[i][j] = d[i][j] - (d[i][k] * d[j][k]) * ratio

        def forward(value):
            out = []
            for k in range(8):
                x = value[k]
                for j in range(k):
                    x = x - low[k][j] * out[j]
                out.append(x * scale[k])
            return out

        inside = (lane >= base) & (lane < base + 8)
        own = jnp.where(inside, jnp.where(lane - base == sub, 1.0, 0.0), a[g])
        r = forward([row(own, k) for k in range(8)])
        w = [None] * 8
        if g + 2 < groups:
            for k in reversed(range(8)):
                x = r[k]
                for j in range(k + 1, 8):
                    x = x - low[j][k] * w[j]
                w[k] = x * scale[k]
        for h in range(g + 1, groups):
            c = [column(a[h], base + k) for k in range(8)]
            if h == g + 1:
                c = forward(c)
            x = jnp.where(inside, 0.0, a[h])
            for k in range(8):
                x = x - c[k] * (r if h == g + 1 else w)[k]
            a[h] = x
        rows = r[0]
        for k in range(1, 8):
            rows = jnp.where(sub == k, r[k], rows)
        done.append(jnp.where(lane <= sub + base, rows, 0.0))
    return done


def factor_kernel(meta, mine, other, out, w, inv, flat):
    n = w.shape[0]
    nb = n // Y
    groups = mine.shape[0]
    tall = flat.shape[0] // (2 * groups)
    for which, half in ((mine, meta[1]), (other, 1 - meta[1])):
        for p in range(groups):
            at = pl.multiple_of((half * groups + p) * tall, 8)
            flat[pl.ds(at, tall), :] = which[p, 0:tall, :]
    at = 0
    for a in range(Y):
        for b in range(a, Y):
            block = flat[at : at + nb, :]
            w[a * nb : (a + 1) * nb, b * nb : (b + 1) * nb] = block
            if a != b:
                w[b * nb : (b + 1) * nb, a * nb : (a + 1) * nb] = block.T
            at += nb
    def trail(p, l21, r12):
        lo, hi = p * nb, (p + 1) * nb
        w[hi:n, hi:n] = w[hi:n, hi:n] - dot(l21, r12, precision=HI)
        new = dot(l21, inv[lo:hi, 0:hi], precision=HI)
        if p:
            inv[hi:n, 0:lo] = inv[hi:n, 0:lo] - new[:, 0:lo]
        inv[hi:n, lo:hi] = -new[:, lo:hi]

    diag = w[0:nb, 0:nb]
    held = None
    for p in range(Y):
        lo, hi = p * nb, (p + 1) * nb
        li = jnp.concatenate(
            eliminate([diag[8 * g : 8 * g + 8, :] for g in range(nb // 8)]), axis=0
        )
        if held:
            trail(p - 1, *held)
            inv[lo:hi, 0:lo] = dot(li, inv[lo:hi, 0:lo], precision=HI)
        inv[lo:hi, lo:hi] = li
        if hi < n:
            inv[lo:hi, hi:n] = jnp.zeros((nb, n - hi), F32)
            held = (dot(w[hi:n, lo:hi], li, 1, 1, HI), dot(li, w[lo:hi, hi:n], precision=HI))
            diag = w[hi : hi + nb, hi : hi + nb] - dot(held[0][0:nb], held[1][:, 0:nb], precision=HI)
    out[...] = inv[...].astype(BF16)


def factor_of(meta, mine, other):
    width = mine.shape[2]
    k = Y * width
    return pl.pallas_call(
        factor_kernel,
        out_shape=shape((k, k), BF16),
        grid_spec=pltpu.PrefetchScalarGridSpec(
            num_scalar_prefetch=1,
            in_specs=[vmem()] * 2,
            out_specs=vmem(),
            scratch_shapes=[
                pltpu.VMEM((k, k), F32),
                pltpu.VMEM((k, k), F32),
                pltpu.VMEM((Y * (Y + 1) // 2 * width, width), F32),
            ],
        ),
        cost_estimate=cost(k * k * k, 12 * k * k),
        compiler_params=pltpu.CompilerParams(vmem_limit_bytes=LIMIT),
        name="factor",
    )(meta, mine, other)


def ortho_kernel(meta, linv, wide, *refs):
    outs, full = refs[:Y], refs[Y]
    width = outs[0].shape[1]
    full[...] = dot(wide[...], linv[...], 1, 1).astype(BF16)
    for t in range(Y):
        at = pl.multiple_of(lax.rem(meta[0] + t, Y) * width, width)
        outs[t][...] = full[:, pl.ds(at, width)]


def ortho_of(meta, linv, wide):
    rows, k = wide.shape
    width = k // Y
    return pl.pallas_call(
        ortho_kernel,
        out_shape=[shape((rows, width), BF16)] * Y,
        grid_spec=pltpu.PrefetchScalarGridSpec(
            num_scalar_prefetch=1,
            in_specs=[vmem()] * 2,
            out_specs=[vmem()] * Y,
            scratch_shapes=[pltpu.VMEM((rows, k), BF16)],
        ),
        cost_estimate=cost(2 * rows * k * k, 4 * rows * k),
        compiler_params=pltpu.CompilerParams(vmem_limit_bytes=LIMIT),
        name="ortho",
    )(meta, linv, wide)


def join_kernel(meta, *refs):
    parts, out = refs[:Y], refs[Y]
    rows = parts[0].shape[0]
    for t in range(Y):
        at = pl.multiple_of(lax.rem(meta[0] + Y - t, Y) * rows, rows)
        out[pl.ds(at, rows), :] = parts[t][...]


def join(meta, parts):
    rows, width = parts[0].shape
    return pl.pallas_call(
        join_kernel,
        out_shape=shape((Y * rows, width), BF16),
        grid_spec=pltpu.PrefetchScalarGridSpec(
            num_scalar_prefetch=1, in_specs=[vmem()] * Y, out_specs=vmem()
        ),
        cost_estimate=cost(0, 4 * Y * rows * width),
        compiler_params=pltpu.CompilerParams(vmem_limit_bytes=LIMIT),
        name="join",
    )(meta, *parts)


def thirds(x):
    a = x.astype(BF16)
    x = x - a.astype(F32)
    b = x.astype(BF16)
    return a, b, (x - b.astype(F32)).astype(BF16)


def tail_kernel(meta, linv, moment, out):
    q, width = out.shape
    rows = linv[pl.ds(pl.multiple_of(meta[0] * width, width), width), :]
    out[...] = sum(
        dot(part, rows[:, d * width : (d + 1) * width], 1, 1)
        for d in range(Y)
        for part in thirds(moment[d * q : (d + 1) * q, :])
    )


def tail_of(meta, linv, moment):
    rows, width = moment.shape
    return pl.pallas_call(
        tail_kernel,
        out_shape=shape((rows // Y, width), F32),
        grid_spec=pltpu.PrefetchScalarGridSpec(
            num_scalar_prefetch=1, in_specs=[vmem()] * 2, out_specs=vmem()
        ),
        cost_estimate=cost(6 * rows * width * width, 2 * linv.size),
        name="tail",
    )(meta, linv, moment)


def project_kernel(meta, linv, mine, other, out, full):
    groups, q, _ = mine.shape
    for which, half in ((mine, meta[1]), (other, 1 - meta[1])):
        for p in range(groups):
            full[pl.ds(pl.multiple_of((half * groups + p) * q, q), q), :] = which[p]
    out[...] = sum(dot(linv[...], part) for part in thirds(full[...]))


def project_of(meta, linv, mine, other):
    k = linv.shape[0]
    width = k // Y
    return pl.pallas_call(
        project_kernel,
        out_shape=shape((k, width), F32),
        grid_spec=pltpu.PrefetchScalarGridSpec(
            num_scalar_prefetch=1,
            in_specs=[vmem()] * 3,
            out_specs=vmem(),
            scratch_shapes=[pltpu.VMEM((k, width), F32)],
        ),
        cost_estimate=cost(6 * k * k * width, 4 * k * k),
        name="project",
    )(meta, linv, mine, other)


def shards(basis, lower, diag, upper, inverse):
    count, size, _ = diag.shape
    r = lax.axis_index("rows")
    c = lax.axis_index("cols")
    meta = jnp.stack([c, lax.rem(r, CORE)]).astype(jnp.int32)

    rows = X * Z * CORE
    forward = [(i, i + 1) for i in range(rows - 1)]
    low = lax.ppermute(basis[-size:], "rows", forward)
    high = lax.ppermute(basis[:size], "rows", [(b, a) for a, b in forward])

    mats = (lower, diag, upper, inverse)
    work = {j: op_chunk(meta, basis, low, high, *mats, j) for j in (2, 1, 3, 0)}
    near = [work[0]] + [along_cols(work[s], s) for s in (1, 2, 3)]
    wide, top, bottom, keep, send = gram_of(meta, near, size)

    half = keep + flip(send)
    gram = total_of(half.reshape(X * Z, -1, half.shape[1]))
    linv = factor_of(meta, *gathered(gram))
    parts = ortho_of(meta, linv, wide)
    ortho = join(meta, [parts[0]] + [along_cols(parts[t], t) for t in (1, 2, 3)])

    before = chain(bottom, 1)
    after = chain(top, -1)
    keep, send = moment_of(meta, wide, before, after, *mats)
    moment = total_of(pack(keep, flip(send)))
    projected = project_of(meta, linv, *gathered(tail_of(meta, linv, moment)))
    return ortho, projected


def solution(mesh):
    in_specs = (
        P("rows", "cols"),
        P("rows", None, None),
        P("rows", None, None),
        P("rows", None, None),
        P("rows", None, None),
    )
    out_specs = (P("rows", "cols"), P(None, "cols"))
    return jax.shard_map(shards, mesh=mesh, in_specs=in_specs, out_specs=out_specs, check_vma=False)
```

```python
import functools

import jax
import jax.numpy as jnp
from jax import lax
from jax.experimental import pallas as pl
from jax.experimental.pallas import tpu as pltpu
from jax.sharding import PartitionSpec as P

F32 = jnp.float32
BF16 = jnp.bfloat16
HI = lax.Precision.HIGHEST
X, Z, CORE, Y = 4, 4, 2, 4
PARTS = 4
LIMIT = 24 << 20
WHOLE = 56 << 20


def dot(a, b, ca=1, cb=0, precision=None):
    return lax.dot_general(
        a, b, (((ca,), (cb,)), ((), ())), precision=precision, preferred_element_type=F32
    )


def cost(flops, bytes_accessed):
    return pl.CostEstimate(flops=flops, transcendentals=0, bytes_accessed=bytes_accessed)


def vmem():
    return pl.BlockSpec(memory_space=pltpu.VMEM)


def shape(dims, dtype):
    return jax.ShapeDtypeStruct(dims, dtype)


def over_rows(move):
    pairs = []
    for x in range(X):
        for z in range(Z):
            for core in range(CORE):
                tx, tz, tc = move(x, z, core)
                source = (x * Z + z) * CORE + core
                pairs.append((source, ((tx % X) * Z + tz % Z) * CORE + tc % CORE))
    return pairs


def flip(value):
    return lax.ppermute(value, "rows", over_rows(lambda x, z, c: (x, z, c + 1)))


PLANE = [[(x * Z + z) * CORE + c for x in range(X) for z in range(Z)] for c in range(CORE)]


def plane(value):
    return lax.all_to_all(value, "rows", 0, 0, tiled=True, axis_index_groups=PLANE)


def along_cols(value, s):
    return lax.ppermute(value, "cols", [(i, (i + s) % Y) for i in range(Y)])


def chain(value, step):
    count = X * Z * CORE * Y
    return lax.ppermute(
        value,
        ("rows", "cols"),
        [(i, i + step) for i in range(count) if 0 <= i + step < count],
    )


def total_of(pieces):
    total = jnp.sum(plane(pieces).astype(F32), axis=0)
    r1, r2, r3 = (along_cols(total, s) for s in (1, 2, 3))
    return (total + r2) + (r1 + r3)


def gathered(piece):
    mine = plane(jnp.broadcast_to(piece[None], (X * Z, *piece.shape)))
    return mine, flip(mine)


def pack_kernel(keep, got, out):
    groups, rows, width = out.shape
    q = rows // Y
    for p in range(groups):
        for d in range(Y):
            at = slice(d * width, (d + 1) * width)
            out[p, d * q : (d + 1) * q, :] = (
                keep[p * q : (p + 1) * q, at] + got[p * q : (p + 1) * q, at]
            ).astype(out.dtype)


def pack(keep, got):
    groups = X * Z
    width = keep.shape[1] // Y
    return pl.pallas_call(
        pack_kernel,
        out_shape=shape((groups, keep.shape[0] * Y // groups, width), BF16),
        in_specs=[vmem()] * 2,
        out_specs=vmem(),
        cost_estimate=cost(keep.size, 12 * keep.size),
        name="pack",
    )(keep, got)


def apply_blocks(v, lower, diag, upper, inverse, out):
    count, size, _ = diag.shape
    mixed = [
        (dot(lower[k], v[k]) + dot(diag[k], v[k + 1]) + dot(upper[k], v[k + 2])).astype(BF16)
        for k in range(count)
    ]
    for k in range(count):
        out[k * size : (k + 1) * size, :] = dot(inverse[k], mixed[k]).astype(BF16)


def op_kernel(meta, prev, cur, nxt, low, high, lower, diag, upper, inverse, out, *, j, per, count):
    size = diag.shape[1]
    first = lax.rem(meta[0] + j, Y) * (count // Y) + pl.program_id(0) * per
    v = [jnp.where(first == 0, low[...], prev[...])]
    v += [cur[k * size : (k + 1) * size, :] for k in range(per)]
    v += [jnp.where(first + per == count, high[...], nxt[...])]
    apply_blocks(v, lower, diag, upper, inverse, out)


def op_chunk(meta, basis, low, high, lower, diag, upper, inverse, j):
    count, size, _ = diag.shape
    width = basis.shape[1]
    per = 4
    steps = count // Y // per

    def block(i, m):
        return lax.rem(m[0] + j, Y) * steps + i

    def at(i, m):
        return (block(i, m), 0)

    def weights(i, m):
        return (block(i, m), 0, 0)

    mat = pl.BlockSpec((per, size, size), weights)
    return pl.pallas_call(
        functools.partial(op_kernel, j=j, per=per, count=count),
        out_shape=shape((count // Y * size, width), BF16),
        grid_spec=pltpu.PrefetchScalarGridSpec(
            num_scalar_prefetch=1,
            grid=(steps,),
            in_specs=[
                pl.BlockSpec((size, width), lambda i, m: (jnp.maximum(block(i, m) * per - 1, 0), 0)),
                pl.BlockSpec((per * size, width), at),
                pl.BlockSpec(
                    (size, width), lambda i, m: (jnp.minimum(block(i, m) * per + per, count - 1), 0)
                ),
                pl.BlockSpec((size, width), lambda i, m: (0, 0)),
                pl.BlockSpec((size, width), lambda i, m: (0, 0)),
                mat,
                mat,
                mat,
                mat,
            ],
            out_specs=pl.BlockSpec((per * size, width), lambda i, m: (i, 0)),
        ),
        cost_estimate=cost(8 * size * size * width * count // Y, 10 * size * size * count // Y),
        compiler_params=pltpu.CompilerParams(vmem_limit_bytes=WHOLE),
        name=f"op{j}",
    )(meta, basis, basis, basis, low, high, lower, diag, upper, inverse)


def gram_kernel(meta, p0, p1, p2, p3, wide, top, bottom, keep, send, full, flat, *, size):
    width = p0.shape[1]
    for s, piece in enumerate((p0, p1, p2, p3)):
        at = lax.rem(meta[0] + Y - s, Y) * width
        wide[:, pl.ds(pl.multiple_of(at, width), width)] = piece[...]
    rows = wide.shape[0]
    top[...] = wide[0:size, :]
    bottom[...] = wide[rows - size : rows, :]
    full[...] = dot(wide[...], wide[...], 0, 0)
    n = 0
    for a in range(Y):
        for b in range(a, Y):
            flat[n * width : (n + 1) * width, :] = full[
                a * width : (a + 1) * width, b * width : (b + 1) * width
            ]
            n += 1
    half = flat.shape[0] // 2
    core = meta[1]
    keep[...] = flat[pl.ds(pl.multiple_of(core * half, 8), half), :]
    send[...] = flat[pl.ds(pl.multiple_of((1 - core) * half, 8), half), :]


def gram_of(meta, pieces, size):
    rows, width = pieces[0].shape
    k = Y * width
    n = Y * (Y + 1) // 2 * width
    return pl.pallas_call(
        functools.partial(gram_kernel, size=size),
        out_shape=(
            shape((rows, k), BF16),
            shape((size, k), BF16),
            shape((size, k), BF16),
            shape((n // 2, width), F32),
            shape((n // 2, width), F32),
        ),
        grid_spec=pltpu.PrefetchScalarGridSpec(
            num_scalar_prefetch=1,
            in_specs=[vmem()] * 4,
            out_specs=(vmem(),) * 5,
            scratch_shapes=[pltpu.VMEM((k, k), F32), pltpu.VMEM((n, width), F32)],
        ),
        cost_estimate=cost(2 * rows * k * k, 4 * rows * k + 4 * k * k),
        compiler_params=pltpu.CompilerParams(vmem_limit_bytes=LIMIT),
        name="gram",
    )(meta, *pieces)


def moment_kernel(meta, prev, cur, nxt, low, high, lower, diag, upper, inverse, keep, send, acc, image):
    i = pl.program_id(0)
    last = pl.num_programs(0) - 1
    per, size, _ = diag.shape
    v = [jnp.where(i == 0, low[...], prev[...])]
    v += [cur[k * size : (k + 1) * size, :] for k in range(per)]
    v += [jnp.where(i == last, high[...], nxt[...])]
    apply_blocks(v, lower, diag, upper, inverse, image)
    term = dot(cur[...], image[...], 0, 0)

    @pl.when(i == 0)
    def _():
        acc[...] = term

    @pl.when(i > 0)
    def _():
        acc[...] += term

    @pl.when(i == last)
    def _():
        half = acc.shape[0] // 2
        core = meta[1]
        keep[...] = acc[pl.ds(pl.multiple_of(core * half, 8), half), :]
        send[...] = acc[pl.ds(pl.multiple_of((1 - core) * half, 8), half), :].astype(BF16)


def moment_of(meta, wide, low, high, lower, diag, upper, inverse):
    count, size, _ = diag.shape
    per = 4
    steps = count // Y // per
    blocks = steps * per
    k = wide.shape[1]
    mat = pl.BlockSpec((per, size, size), lambda i, m: (m[0] * steps + i, 0, 0))
    out = pl.BlockSpec((k // 2, k), lambda i, m: (0, 0))
    return pl.pallas_call(
        moment_kernel,
        out_shape=(shape((k // 2, k), F32), shape((k // 2, k), BF16)),
        grid_spec=pltpu.PrefetchScalarGridSpec(
            num_scalar_prefetch=1,
            grid=(steps,),
            in_specs=[
                pl.BlockSpec((size, k), lambda i, m: (jnp.maximum(i * per - 1, 0), 0)),
                pl.BlockSpec((per * size, k), lambda i, m: (i, 0)),
                pl.BlockSpec((size, k), lambda i, m: (jnp.minimum(i * per + per, blocks - 1), 0)),
                pl.BlockSpec((size, k), lambda i, m: (0, 0)),
                pl.BlockSpec((size, k), lambda i, m: (0, 0)),
                mat,
                mat,
                mat,
                mat,
            ],
            out_specs=(out, out),
            scratch_shapes=[pltpu.VMEM((k, k), F32), pltpu.VMEM((per * size, k), BF16)],
        ),
        cost_estimate=cost(blocks * size * k * (8 * size + 2 * k), 4 * blocks * size * k),
        compiler_params=pltpu.CompilerParams(vmem_limit_bytes=WHOLE),
        name="moment",
    )(meta, wide, wide, wide, low, high, lower, diag, upper, inverse)


def eliminate(a):
    groups = len(a)
    wide = (8, 8 * groups)
    sub = lax.broadcasted_iota(jnp.int32, wide, 0)
    lane = lax.broadcasted_iota(jnp.int32, wide, 1)
    a = list(a)

    def column(value, k):
        return jnp.broadcast_to(value[:, k : k + 1], wide)

    def row(value, k):
        return jnp.broadcast_to(value[k : k + 1, :], wide)

    done = []
    for g in range(groups):
        base = 8 * g
        cols = [column(a[g], base + k) for k in range(8)]
        d = [[row(cols[k], i) if i >= k else None for k in range(8)] for i in range(8)]
        low = [[None] * 8 for _ in range(8)]
        scale = [None] * 8
        for k in range(8):
            scale[k] = lax.rsqrt(d[k][k])
            ratio = 1.0 / d[k][k]
            for i in range(k + 1, 8):
                low[i][k] = d[i][k] * scale[k]
                for j in range(k + 1, i + 1):
                    d[i][j] = d[i][j] - (d[i][k] * d[j][k]) * ratio

        def forward(value):
            out = []
            for k in range(8):
                x = value[k]
                for j in range(k):
                    x = x - low[k][j] * out[j]
                out.append(x * scale[k])
            return out

        inside = (lane >= base) & (lane < base + 8)
        own = jnp.where(inside, jnp.where(lane - base == sub, 1.0, 0.0), a[g])
        r = forward([row(own, k) for k in range(8)])
        w = [None] * 8
        if g + 2 < groups:
            for k in reversed(range(8)):
                x = r[k]
                for j in range(k + 1, 8):
                    x = x - low[j][k] * w[j]
                w[k] = x * scale[k]
        for h in range(g + 1, groups):
            c = [column(a[h], base + k) for k in range(8)]
            if h == g + 1:
                c = forward(c)
            x = jnp.where(inside, 0.0, a[h])
            for k in range(8):
                x = x - c[k] * (r if h == g + 1 else w)[k]
            a[h] = x
        rows = r[0]
        for k in range(1, 8):
            rows = jnp.where(sub == k, r[k], rows)
        done.append(jnp.where(lane <= sub + base, rows, 0.0))
    return done


def factor_kernel(meta, mine, other, out, w, inv, flat):
    n = w.shape[0]
    nb = n // Y
    groups = mine.shape[0]
    tall = flat.shape[0] // (2 * groups)
    for which, half in ((mine, meta[1]), (other, 1 - meta[1])):
        for p in range(groups):
            at = pl.multiple_of((half * groups + p) * tall, 8)
            flat[pl.ds(at, tall), :] = which[p, 0:tall, :]
    at = 0
    for a in range(Y):
        for b in range(a, Y):
            block = flat[at : at + nb, :]
            w[a * nb : (a + 1) * nb, b * nb : (b + 1) * nb] = block
            if a != b:
                w[b * nb : (b + 1) * nb, a * nb : (a + 1) * nb] = block.T
            at += nb
    def trail(p, l21, r12):
        lo, hi = p * nb, (p + 1) * nb
        w[hi:n, hi:n] = w[hi:n, hi:n] - dot(l21, r12, precision=HI)
        new = dot(l21, inv[lo:hi, 0:hi], precision=HI)
        if p:
            inv[hi:n, 0:lo] = inv[hi:n, 0:lo] - new[:, 0:lo]
        inv[hi:n, lo:hi] = -new[:, lo:hi]

    diag = w[0:nb, 0:nb]
    held = None
    for p in range(Y):
        lo, hi = p * nb, (p + 1) * nb
        li = jnp.concatenate(
            eliminate([diag[8 * g : 8 * g + 8, :] for g in range(nb // 8)]), axis=0
        )
        if held:
            trail(p - 1, *held)
            inv[lo:hi, 0:lo] = dot(li, inv[lo:hi, 0:lo], precision=HI)
        inv[lo:hi, lo:hi] = li
        if hi < n:
            inv[lo:hi, hi:n] = jnp.zeros((nb, n - hi), F32)
            held = (dot(w[hi:n, lo:hi], li, 1, 1, HI), dot(li, w[lo:hi, hi:n], precision=HI))
            diag = w[hi : hi + nb, hi : hi + nb] - dot(held[0][0:nb], held[1][:, 0:nb], precision=HI)
    out[...] = inv[...].astype(BF16)


def factor_of(meta, mine, other):
    width = mine.shape[2]
    k = Y * width
    return pl.pallas_call(
        factor_kernel,
        out_shape=shape((k, k), BF16),
        grid_spec=pltpu.PrefetchScalarGridSpec(
            num_scalar_prefetch=1,
            in_specs=[vmem()] * 2,
            out_specs=vmem(),
            scratch_shapes=[
                pltpu.VMEM((k, k), F32),
                pltpu.VMEM((k, k), F32),
                pltpu.VMEM((Y * (Y + 1) // 2 * width, width), F32),
            ],
        ),
        cost_estimate=cost(k * k * k, 12 * k * k),
        compiler_params=pltpu.CompilerParams(vmem_limit_bytes=LIMIT),
        name="factor",
    )(meta, mine, other)


def ortho_kernel(meta, linv, wide, *refs):
    outs, full = refs[:Y], refs[Y]
    width = outs[0].shape[1]
    full[...] = dot(wide[...], linv[...], 1, 1).astype(BF16)
    for t in range(Y):
        at = pl.multiple_of(lax.rem(meta[0] + t, Y) * width, width)
        outs[t][...] = full[:, pl.ds(at, width)]


def ortho_of(meta, linv, wide):
    rows, k = wide.shape
    width = k // Y
    return pl.pallas_call(
        ortho_kernel,
        out_shape=[shape((rows, width), BF16)] * Y,
        grid_spec=pltpu.PrefetchScalarGridSpec(
            num_scalar_prefetch=1,
            in_specs=[vmem()] * 2,
            out_specs=[vmem()] * Y,
            scratch_shapes=[pltpu.VMEM((rows, k), BF16)],
        ),
        cost_estimate=cost(2 * rows * k * k, 4 * rows * k),
        compiler_params=pltpu.CompilerParams(vmem_limit_bytes=LIMIT),
        name="ortho",
    )(meta, linv, wide)


def join_kernel(meta, *refs):
    parts, out = refs[:Y], refs[Y]
    rows = parts[0].shape[0]
    for t in range(Y):
        at = pl.multiple_of(lax.rem(meta[0] + Y - t, Y) * rows, rows)
        out[pl.ds(at, rows), :] = parts[t][...]


def join(meta, parts):
    rows, width = parts[0].shape
    return pl.pallas_call(
        join_kernel,
        out_shape=shape((Y * rows, width), BF16),
        grid_spec=pltpu.PrefetchScalarGridSpec(
            num_scalar_prefetch=1, in_specs=[vmem()] * Y, out_specs=vmem()
        ),
        cost_estimate=cost(0, 4 * Y * rows * width),
        compiler_params=pltpu.CompilerParams(vmem_limit_bytes=LIMIT),
        name="join",
    )(meta, *parts)


def thirds(x):
    a = x.astype(BF16)
    x = x - a.astype(F32)
    b = x.astype(BF16)
    return a, b, (x - b.astype(F32)).astype(BF16)


def tail_kernel(meta, linv, moment, out):
    q, width = out.shape
    rows = linv[pl.ds(pl.multiple_of(meta[0] * width, width), width), :]
    out[...] = sum(
        dot(part, rows[:, d * width : (d + 1) * width], 1, 1)
        for d in range(Y)
        for part in thirds(moment[d * q : (d + 1) * q, :])
    )


def tail_of(meta, linv, moment):
    rows, width = moment.shape
    return pl.pallas_call(
        tail_kernel,
        out_shape=shape((rows // Y, width), F32),
        grid_spec=pltpu.PrefetchScalarGridSpec(
            num_scalar_prefetch=1, in_specs=[vmem()] * 2, out_specs=vmem()
        ),
        cost_estimate=cost(6 * rows * width * width, 2 * linv.size),
        name="tail",
    )(meta, linv, moment)


def project_kernel(meta, linv, mine, other, out, full):
    groups, q, _ = mine.shape
    for which, half in ((mine, meta[1]), (other, 1 - meta[1])):
        for p in range(groups):
            full[pl.ds(pl.multiple_of((half * groups + p) * q, q), q), :] = which[p]
    out[...] = sum(dot(linv[...], part) for part in thirds(full[...]))


def project_of(meta, linv, mine, other):
    k = linv.shape[0]
    width = k // Y
    return pl.pallas_call(
        project_kernel,
        out_shape=shape((k, width), F32),
        grid_spec=pltpu.PrefetchScalarGridSpec(
            num_scalar_prefetch=1,
            in_specs=[vmem()] * 3,
            out_specs=vmem(),
            scratch_shapes=[pltpu.VMEM((k, width), F32)],
        ),
        cost_estimate=cost(6 * k * k * width, 4 * k * k),
        name="project",
    )(meta, linv, mine, other)


def shards(basis, lower, diag, upper, inverse):
    count, size, _ = diag.shape
    r = lax.axis_index("rows")
    c = lax.axis_index("cols")
    meta = jnp.stack([c, lax.rem(r, CORE)]).astype(jnp.int32)

    rows = X * Z * CORE
    forward = [(i, i + 1) for i in range(rows - 1)]
    low = lax.ppermute(basis[-size:], "rows", forward)
    high = lax.ppermute(basis[:size], "rows", [(b, a) for a, b in forward])

    mats = (lower, diag, upper, inverse)
    work = {j: op_chunk(meta, basis, low, high, *mats, j) for j in (2, 1, 3, 0)}
    near = [work[0]] + [along_cols(work[s], s) for s in (1, 2, 3)]
    wide, top, bottom, keep, send = gram_of(meta, near, size)

    half = keep + flip(send)
    gram = total_of(half.reshape(X * Z, -1, half.shape[1]))
    linv = factor_of(meta, *gathered(gram))
    parts = ortho_of(meta, linv, wide)
    ortho = join(meta, [parts[0]] + [along_cols(parts[t], t) for t in (1, 2, 3)])

    before = chain(bottom, 1)
    after = chain(top, -1)
    keep, send = moment_of(meta, wide, before, after, *mats)
    moment = total_of(pack(keep, flip(send)))
    projected = project_of(meta, linv, *gathered(tail_of(meta, linv, moment)))
    return ortho, projected


def solution(mesh):
    in_specs = (
        P("rows", "cols"),
        P("rows", None, None),
        P("rows", None, None),
        P("rows", None, None),
        P("rows", None, None),
    )
    out_specs = (P("rows", "cols"), P(None, "cols"))
    return jax.shard_map(shards, mesh=mesh, in_specs=in_specs, out_specs=out_specs, check_vma=False)
```
